128 devices in a mesh: snap: 16 (over x_lo, y, core), clus: 8 (over z, x_hi).
Axes of the slice: x: 4 (x_hi: 2, x_lo: 2; x = x_hi * 2 + x_lo), y: 4, z: 4, core: 2. Of those that a mesh axis runs over, the one named last changes fastest.
Arguments:
- features: bfloat16 [64, 4096, 512], P('snap', 'clus'), parts along dimension 1, may hold values from -6 to 6
- adjacency: int32 [64, 4096, 512], P('snap', 'clus'), parts along dimension 1, may hold values 0 or 1
- first_seen: int32 [4096], P(('clus', 'snap')), parts along dimension 0, may hold values from 0 to 31
- pos_embed: bfloat16 [64, 512], replicated, may hold values from -3 to 3
- w_struct: bfloat16 [2, 512, 512], replicated, may hold values from -0.25 to 0.25
- w_query: bfloat16 [2, 512, 512], replicated, as said below
- w_key: bfloat16 [2, 512, 512], replicated, as said below
- w_value: bfloat16 [2, 512, 512], replicated, may hold values from -0.25 to 0.25
- w_out: bfloat16 [2, 512, 512], replicated, may hold values from -0.25 to 0.25
- w_up: bfloat16 [2, 512, 1024], replicated, may hold values from -0.25 to 0.25
- w_down: bfloat16 [2, 1024, 512], replicated, may hold values from -0.1875 to 0.1875
- norm_gain: float32 [2, 2, 512], replicated, may hold values from 0.1 to 1.9
Outputs:
- hidden_out: bfloat16 [64, 4096, 512], P('snap', 'clus'), parts along dimension 1
The draws below stay inside these ranges and needn't reach their ends.
There are 8 independent parts, one for each index of `clus`. The reference program is written for one: setup_inputs(seed, part) draws one part's arguments, and reference() takes and returns one part's arrays. A program takes and returns all parts, laid end to end along the dimension named above; an argument that names none is the same for every part. Nothing has to cross between parts.
Inputs may be any that keep to these rules, and one draw needn't show every extreme that they name: `w_query`: entries lie within -30 / sqrt(512) to 30 / sqrt(512). `w_key`: entries lie within -5 / sqrt(512) to 5 / sqrt(512).
All inputs are finite; a program needn't handle non-finite values. No bound on the sum of `adjacency` on one device may be relied on, other than what follows from the above.
Results may differ from the reference program's by a relative error of at most 0.012.
Values may be sent and summed in bfloat16 or wider, within the bound.
No kernel may reach another device: no remote copies, remote signals or barrier semaphores. Data moves between devices by JAX's collectives and lax.ppermute only.
A program may use at most 128 MiB of HBM per device.

```python
import jax
import jax.numpy as jnp
from jax import lax

D = 512
FF = 1024
HEADS = 8
NODES = 512
BLOCKS = 2
S = 64


def paired_projections(key):
    base_key = jax.random.fold_in(key, 7031)
    key_part = jax.random.normal(jax.random.fold_in(base_key, 1), (BLOCKS, D, D), jnp.float32)
    noise_part = jax.random.normal(jax.random.fold_in(base_key, 2), (BLOCKS, D, D), jnp.float32)
    key_part = jnp.clip(key_part, -5.0, 5.0) * D ** (-0.5)
    noise_part = jnp.clip(noise_part, -5.0, 5.0) * D ** (-0.5)
    query_part = noise_part
    return (query_part, key_part)


def draw_w_query(key, part):
    return paired_projections(key)[0].astype(jnp.bfloat16)


def draw_w_key(key, part):
    return paired_projections(key)[1].astype(jnp.bfloat16)


def plant(entries, key, smallest, largest):
    place = [jax.random.randint(jax.random.fold_in(key, axis), (), 0, length) for axis, length in enumerate(entries.shape)]
    main_axis = entries.shape.index(max(entries.shape))
    neighbour = place[:main_axis] + [(place[main_axis] + 1) % entries.shape[main_axis]] + place[main_axis + 1:]
    return entries.at[tuple(place)].set(smallest).at[tuple(neighbour)].set(largest)


def steps_of(key, shape, split, least, largest):
    level, own = 1.0, jax.random.fold_in(key, 6)
    for axis_at, parts in split:
        steps = jnp.exp(jax.random.uniform(jax.random.fold_in(own, axis_at), (parts,), jnp.float32, least / len(split), largest / len(split)))
        level = level * jnp.repeat(steps, shape[axis_at] // parts).reshape([-1 if axis == axis_at else 1 for axis in range(len(shape))])
    return level


def bell_draw(stream_key, dims, width, most, shards=(), kind=jnp.bfloat16):
    result = width * jax.random.normal(stream_key, dims, jnp.float32)
    if shards:
        result = result * steps_of(stream_key, dims, shards, -0.22, 0.18)
    return jnp.clip(result, -most, most).astype(kind)


def setup_inputs(seed: int = 0, part: int = 0) -> dict:
    keys = jax.random.split(jax.random.key(seed), 13)
    own_keys = jax.random.split(jax.random.fold_in(keys[12], part), 13)
    return {
        "features": bell_draw(own_keys[0], (S, NODES, D), 1.0, 6.0, ((0, 16),)),
        "adjacency": plant((jax.random.randint(own_keys[1], (S, NODES, NODES), 0, 16) < 1).astype(jnp.int32), jax.random.fold_in(own_keys[1], 1), 0, 1),
        "first_seen": plant(jax.random.randint(own_keys[2], (NODES,), 0, S // 2), jax.random.fold_in(own_keys[2], 1), 0, (S // 2) - 1).astype(jnp.int32),
        "pos_embed": bell_draw(keys[3], (S, D), 0.5, 3.0),
        "w_struct": bell_draw(keys[4], (BLOCKS, D, D), D ** -0.5, 0.25),
        "w_query": draw_w_query(jax.random.fold_in(keys[12], 71), part),
        "w_key": draw_w_key(jax.random.fold_in(keys[12], 71), part),
        "w_value": bell_draw(keys[7], (BLOCKS, D, D), D ** -0.5, 0.25),
        "w_out": bell_draw(keys[8], (BLOCKS, D, D), D ** -0.5, 0.25),
        "w_up": bell_draw(keys[9], (BLOCKS, D, FF), D ** -0.5, 0.25),
        "w_down": bell_draw(keys[10], (BLOCKS, FF, D), FF ** -0.5, 0.1875),
        "norm_gain": jnp.clip(1.0 + 0.18 * jax.random.normal(keys[11], (BLOCKS, 2, D), jnp.float32), 0.1, 1.9),
    }


def layer_norm(values_in, gain):
    average = lax.optimization_barrier(jnp.mean(values_in, axis=-1, keepdims=True))
    centred = values_in - average
    scattered_rows = lax.optimization_barrier(jnp.mean(centred * centred, axis=-1, keepdims=True))
    return centred * lax.rsqrt(scattered_rows + 1e-05) * gain

def structure_output(hidden, adjacent, weight_matrix):
    degree = 1.0 + lax.optimization_barrier(jnp.sum(adjacent, axis=1)).astype(jnp.float32)
    summed = jnp.dot(adjacent.astype(jnp.bfloat16), hidden, preferred_element_type=jnp.float32) + hidden.astype(jnp.float32)
    blended_values = (summed / degree[:, None]).astype(jnp.bfloat16)
    convolved = jax.nn.elu(jnp.dot(blended_values, weight_matrix, preferred_element_type=jnp.float32))
    return (convolved + hidden.astype(jnp.float32)).astype(jnp.bfloat16)

def temporal(vertex_rows, first_seen, pos_embed, w_query, w_key, w_value, w_out, w_up, w_down, gain_pair):
    timestep_count, vertex_count, model_width = vertex_rows.shape
    head_dim = model_width // HEADS
    row_totals = vertex_rows.astype(jnp.float32) + pos_embed.astype(jnp.float32)[:, None, :]
    row_totals = row_totals.reshape(-1, model_width)
    normed = layer_norm(row_totals, gain_pair[0]).astype(jnp.bfloat16)
    shape_heads = (timestep_count, vertex_count, HEADS, head_dim)
    queries = jnp.dot(normed, w_query, preferred_element_type=jnp.float32).astype(jnp.bfloat16).reshape(shape_heads)
    key_rows = jnp.dot(normed, w_key, preferred_element_type=jnp.float32).astype(jnp.bfloat16).reshape(shape_heads)
    values = jnp.dot(normed, w_value, preferred_element_type=jnp.float32).astype(jnp.bfloat16).reshape(shape_heads)
    scores = jnp.einsum('tvhd,jvhd->vhtj', queries.astype(jnp.float32), key_rows.astype(jnp.float32)) * head_dim ** (-0.5)
    positions = jnp.arange(timestep_count, dtype=jnp.int32)
    causal = positions[None, :] <= positions[:, None]
    diagonal_mask = positions[None, :] == positions[:, None]
    present = positions[None, None, :] >= first_seen[:, None, None]
    allowed = causal[None] & (present | diagonal_mask[None])
    scores = jnp.where(allowed[:, None], scores, -1e+30)
    weights = jax.nn.softmax(scores, axis=-1).astype(jnp.bfloat16)
    attended_heads = jnp.einsum('vhtj,jvhd->tvhd', weights.astype(jnp.float32), values.astype(jnp.float32))
    attended_heads = attended_heads.astype(jnp.bfloat16).reshape(-1, model_width)
    attended = row_totals + jnp.dot(attended_heads, w_out, preferred_element_type=jnp.float32)
    normed_two = layer_norm(attended, gain_pair[1]).astype(jnp.bfloat16)
    inner_rows = jax.nn.gelu(jnp.dot(normed_two, w_up, preferred_element_type=jnp.float32)).astype(jnp.bfloat16)
    finished = attended + jnp.dot(inner_rows, w_down, preferred_element_type=jnp.float32)
    return finished.astype(jnp.bfloat16).reshape(timestep_count, vertex_count, model_width)

def reference(features, adjacency, first_seen, pos_embed, w_struct, w_query, w_key, w_value, w_out, w_up, w_down, norm_gain):
    hidden = features
    for layer in range(BLOCKS):
        weight_matrix = w_struct[layer]
        convolved = lax.map(lambda snapshot_pair: structure_output(snapshot_pair[0], snapshot_pair[1], weight_matrix), (hidden, adjacency))
        hidden = temporal(convolved, first_seen, pos_embed, w_query[layer], w_key[layer], w_value[layer], w_out[layer], w_up[layer], w_down[layer], norm_gain[layer])
    return hidden
```

```python
import functools

import jax
import jax.numpy as jnp
from jax import lax
from jax.experimental import pallas as pl
from jax.experimental.pallas import tpu as pltpu
from jax.sharding import PartitionSpec as P

HEADS = 8
BLOCKS = 2
CHUNKS = 2
GROUP = 8
LANES = 128
VMEM_LIMIT = 48 * 1024 * 1024


def normalise(rows, gain):
    average = jnp.mean(rows, axis=-1, keepdims=True)
    centred = rows - average
    spread = jnp.mean(centred * centred, axis=-1, keepdims=True)
    return (centred * lax.rsqrt(spread + 1e-05) * gain).astype(jnp.bfloat16)


def structure_kernel(*refs, pieces, chunk):
    hidden_refs = refs[:pieces]
    adjacency_ref, weight_ref, out_ref, gathered = refs[pieces:]
    owners, _, rows, width = out_ref.shape
    nodes = adjacency_ref.shape[-1]
    part = nodes // owners // pieces
    if pieces == 1:
        hidden = hidden_refs[0][...].reshape(nodes, width)
        own = hidden.reshape(owners, nodes // owners, width)[:, chunk * rows : (chunk + 1) * rows]
    else:
        for piece in range(pieces):
            gathered[:, piece * part : (piece + 1) * part, :] = hidden_refs[piece][:, 0]
        hidden = gathered[...].reshape(nodes, width)
        own = hidden_refs[chunk][:, 0]
    own = own.reshape(owners * rows, width).astype(jnp.float32)
    links = adjacency_ref[...].reshape(owners * rows, nodes).astype(jnp.float32)
    degree = 1.0 + jnp.sum(links, axis=1, keepdims=True)
    summed = jnp.dot(links.astype(jnp.bfloat16), hidden, preferred_element_type=jnp.float32)
    mixture = ((summed + own) / degree).astype(jnp.bfloat16)
    mapped = jnp.dot(mixture, weight_ref[0], preferred_element_type=jnp.float32)
    bent = jnp.where(mapped > 0, mapped, jnp.exp(jnp.minimum(mapped, 0.0)) - 1.0)
    out_ref[...] = (bent + own).astype(jnp.bfloat16).reshape(out_ref.shape)


def structure(hidden, adjacency, w_struct, layer, chunk, owners):
    snapshots, nodes, _ = adjacency.shape
    width = w_struct.shape[-1]
    rows = nodes // owners // CHUNKS
    pieces = len(hidden)
    if pieces == 1:
        hidden_specs = [pl.BlockSpec((1, nodes, width), lambda s: (s, 0, 0))]
    else:
        hidden_specs = [pl.BlockSpec((owners, 1, rows, width), lambda s: (0, s, 0, 0))] * pieces
    links = adjacency.reshape(snapshots, owners, CHUNKS, rows, nodes)
    flops = 2 * snapshots * owners * rows * width * (nodes + width)
    return pl.pallas_call(
        functools.partial(structure_kernel, pieces=pieces, chunk=chunk),
        grid=(snapshots,),
        out_shape=jax.ShapeDtypeStruct((owners, snapshots, rows, width), jnp.bfloat16),
        in_specs=hidden_specs
        + [
            pl.BlockSpec((1, owners, 1, rows, nodes), lambda s: (s, 0, chunk, 0, 0)),
            pl.BlockSpec((1, width, width), lambda s: (layer, 0, 0)),
        ],
        out_specs=pl.BlockSpec((owners, 1, rows, width), lambda s: (0, s, 0, 0)),
        scratch_shapes=[pltpu.VMEM((owners, nodes // owners, width), jnp.bfloat16)],
        compiler_params=pltpu.CompilerParams(vmem_limit_bytes=VMEM_LIMIT),
        cost_estimate=pl.CostEstimate(
            flops=flops, transcendentals=0, bytes_accessed=snapshots * owners * rows * nodes * 8
        ),
        name=f"structure_{layer}_{chunk}",
    )(*hidden, links, w_struct)


def temporal_kernel(
    first_ref,
    x_ref,
    pos_ref,
    wq_ref,
    wk_ref,
    wv_ref,
    wo_ref,
    wu_ref,
    wd_ref,
    gain_ref,
    out_ref,
    mixed,
    rows_sum,
    normed,
    queries,
    key_rows,
    values,
    joined,
    order,
    *,
    first_vertex,
):
    steps, group, width = x_ref.shape
    head_dim = width // HEADS
    pair = 2 * head_dim
    f32 = jnp.float32

    row = lax.broadcasted_iota(jnp.int32, (steps, pair), 0)
    lane = lax.broadcasted_iota(jnp.int32, (steps, pair), 1)
    column = lane & (head_dim - 1)
    order[...] = jnp.where(row < column, row, jnp.where(row == column, 1 << 20, -1))
    left = lane < head_dim

    for tile in range(width // LANES):
        mixed[tile] = (
            x_ref[:, :, tile * LANES : (tile + 1) * LANES]
            .astype(f32)
            .reshape(steps * group, LANES)
        )
    gain_one = gain_ref[0, 0:1, :]
    gain_two = gain_ref[0, 1:2, :]
    pos = pos_ref[...].astype(f32)
    for v in range(group):
        span = slice(v * steps, (v + 1) * steps)
        parts = [mixed[tile, pl.ds(v, steps, stride=group), :] for tile in range(width // LANES)]
        total = jnp.concatenate(parts, axis=1) + pos
        rows_sum[span, :] = total
        normed[span, :] = normalise(total, gain_one)
    rows = normed[...]
    queries[...] = (
        jnp.dot(rows, wq_ref[0], preferred_element_type=f32) * head_dim ** (-0.5)
    ).astype(jnp.bfloat16)
    key_rows[...] = jnp.dot(rows, wk_ref[0], preferred_element_type=f32).astype(jnp.bfloat16)
    values[...] = jnp.dot(rows, wv_ref[0], preferred_element_type=f32).astype(jnp.bfloat16)

    base = first_vertex + pl.program_id(0) * group

    zero = jnp.zeros((steps, pair), jnp.bfloat16)
    for v in range(group):
        first = first_ref[base + v]
        allowed = order[...] >= first
        span = slice(v * steps, (v + 1) * steps)
        for p in range(width // pair):
            lanes = slice(p * pair, (p + 1) * pair)
            q = queries[span, lanes]
            stacked = jnp.concatenate(
                [jnp.where(left, q, zero), jnp.where(left, zero, q)], axis=0
            )
            scores = lax.dot_general(
                key_rows[span, lanes], stacked, (((1,), (1,)), ((), ())), preferred_element_type=f32
            )
            scores = jnp.where(allowed, scores, -1e30)
            top = jnp.max(scores, axis=0, keepdims=True)
            raised = jnp.exp(scores - top)
            weights = (raised * (1.0 / jnp.sum(raised, axis=0, keepdims=True))).astype(jnp.bfloat16)
            both = lax.dot_general(
                weights, values[span, lanes], (((0,), (0,)), ((), ())), preferred_element_type=f32
            )
            joined[span, lanes] = jnp.where(left, both[:steps], both[steps:]).astype(jnp.bfloat16)

    attended = rows_sum[...] + jnp.dot(joined[...], wo_ref[0], preferred_element_type=f32)
    inner = jax.nn.gelu(
        jnp.dot(normalise(attended, gain_two), wu_ref[0], preferred_element_type=f32)
    ).astype(jnp.bfloat16)
    finished = attended + jnp.dot(inner, wd_ref[0], preferred_element_type=f32)
    for tile in range(width // LANES):
        lanes = slice(tile * LANES, (tile + 1) * LANES)
        for v in range(group):
            mixed[tile, pl.ds(v, steps, stride=group), :] = finished[
                v * steps : (v + 1) * steps, lanes
            ]
        out_ref[:, :, lanes] = mixed[tile].reshape(steps, group, LANES).astype(jnp.bfloat16)


def temporal(
    rows, first_seen, pos_embed, w_query, w_key, w_value, w_out, w_up, w_down, norm_gain, layer, chunk
):
    steps, count, width = rows.shape
    inner = w_up.shape[-1]
    group = min(GROUP, count)

    def weight(array):
        return pl.BlockSpec(
            (1,) + array.shape[1:], lambda i: (layer, 0, 0), pipeline_mode=pl.Buffered(1)
        )

    size = steps * group
    flops = 2 * steps * count * width * (4 * width + 2 * inner)
    return pl.pallas_call(
        functools.partial(temporal_kernel, first_vertex=chunk * count),
        grid=(count // group,),
        out_shape=jax.ShapeDtypeStruct(rows.shape, jnp.bfloat16),
        in_specs=[
            pl.BlockSpec(memory_space=pltpu.SMEM),
            pl.BlockSpec((steps, group, width), lambda i: (0, i, 0)),
            pl.BlockSpec(pos_embed.shape, lambda i: (0, 0), pipeline_mode=pl.Buffered(1)),
            weight(w_query),
            weight(w_key),
            weight(w_value),
            weight(w_out),
            weight(w_up),
            weight(w_down),
            weight(norm_gain),
        ],
        out_specs=pl.BlockSpec((steps, group, width), lambda i: (0, i, 0)),
        scratch_shapes=[
            pltpu.VMEM((width // LANES, size, LANES), jnp.float32),
            pltpu.VMEM((size, width), jnp.float32),
            pltpu.VMEM((size, width), jnp.bfloat16),
            pltpu.VMEM((size, width), jnp.bfloat16),
            pltpu.VMEM((size, width), jnp.bfloat16),
            pltpu.VMEM((size, width), jnp.bfloat16),
            pltpu.VMEM((size, width), jnp.bfloat16),
            pltpu.VMEM((steps, 2 * width // HEADS), jnp.int32),
        ],
        compiler_params=pltpu.CompilerParams(vmem_limit_bytes=VMEM_LIMIT),
        cost_estimate=pl.CostEstimate(
            flops=flops, transcendentals=0, bytes_accessed=4 * steps * count * width + 4 * 2**20
        ),
        name=f"temporal_{layer}_{chunk}",
    )(first_seen, rows, pos_embed, w_query, w_key, w_value, w_out, w_up, w_down, norm_gain)


def on_device(
    features,
    adjacency,
    first_seen,
    pos_embed,
    w_struct,
    w_query,
    w_key,
    w_value,
    w_out,
    w_up,
    w_down,
    norm_gain,
    *,
    owners,
):
    snapshots, nodes, width = features.shape

    def exchange(array):
        return lax.all_to_all(array, "snap", split_axis=0, concat_axis=0, tiled=True)

    hidden = (features,)
    for layer in range(BLOCKS):
        arrived = [
            exchange(structure(hidden, adjacency, w_struct, layer, chunk, owners))
            for chunk in range(CHUNKS)
        ]
        hidden = []
        for chunk in range(CHUNKS):
            rows = arrived[chunk].shape[2]
            finished = temporal(
                arrived[chunk].reshape(owners * snapshots, rows, width),
                first_seen,
                pos_embed,
                w_query,
                w_key,
                w_value,
                w_out,
                w_up,
                w_down,
                norm_gain,
                layer,
                chunk,
            )
            hidden.append(exchange(finished.reshape(owners, snapshots, rows, width)))
    joined = jnp.concatenate(hidden, axis=2)
    return joined.transpose(1, 0, 2, 3).reshape(snapshots, nodes, width)


def solution(mesh):
    in_specs = (
        P("snap", "clus", None),
        P("snap", "clus", None),
        P(("clus", "snap")),
        P(),
        P(),
        P(),
        P(),
        P(),
        P(),
        P(),
        P(),
        P(),
    )
    out_specs = P("snap", "clus", None)
    return jax.shard_map(
        functools.partial(on_device, owners=mesh.shape["snap"]),
        mesh=mesh,
        in_specs=in_specs,
        out_specs=out_specs,
        check_vma=False,
    )
```

```python
import functools

import jax
import jax.numpy as jnp
from jax import lax
from jax.experimental import pallas as pl
from jax.experimental.pallas import tpu as pltpu
from jax.sharding import PartitionSpec as P

HEADS = 8
BLOCKS = 2
GROUP = 8
LANES = 128
LEAD_QUARTERS = 3
VMEM_LIMIT = 40 * 1024 * 1024


def in_hbm(array):
    return pltpu.with_memory_space_constraint(array, pltpu.HBM)


def normalise(rows, gain):
    average = jnp.mean(rows, axis=-1, keepdims=True)
    centred = rows - average
    spread = jnp.mean(centred * centred, axis=-1, keepdims=True)
    return (centred * lax.rsqrt(spread + 1e-05) * gain).astype(jnp.bfloat16)


def structure_kernel(hidden_ref, adjacency_ref, weight_ref, out_ref, *, start):
    owners, _, rows, width = out_ref.shape
    nodes = adjacency_ref.shape[-1]
    hidden = hidden_ref[...].reshape(nodes, width)
    own = hidden.reshape(owners, nodes // owners, width)[:, start : start + rows]
    own = own.reshape(owners * rows, width).astype(jnp.float32)
    links = adjacency_ref[0, :, start : start + rows, :]
    links = links.reshape(owners * rows, nodes).astype(jnp.float32)
    degree = 1.0 + jnp.sum(links, axis=1, keepdims=True)
    summed = jnp.dot(links.astype(jnp.bfloat16), hidden, preferred_element_type=jnp.float32)
    mixture = ((summed + own) / degree).astype(jnp.bfloat16)
    mapped = jnp.dot(mixture, weight_ref[0], preferred_element_type=jnp.float32)
    bent = jnp.where(mapped > 0, mapped, jnp.exp(jnp.minimum(mapped, 0.0)) - 1.0)
    out_ref[...] = (bent + own).astype(jnp.bfloat16).reshape(out_ref.shape)


def structure(hidden, adjacency, w_struct, layer, start, rows, owners):
    snapshots, nodes, _ = adjacency.shape
    width = w_struct.shape[-1]
    share = nodes // owners
    if hidden.ndim == 3:
        hidden_spec = pl.BlockSpec((1, nodes, width), lambda s: (s, 0, 0))
    else:
        hidden_spec = pl.BlockSpec((owners, 1, share, width), lambda s: (0, s, 0, 0))
    links = adjacency.reshape(snapshots, owners, share, nodes)
    flops = 2 * snapshots * owners * rows * width * (nodes + width)
    return pl.pallas_call(
        functools.partial(structure_kernel, start=start),
        grid=(snapshots,),
        out_shape=pltpu.HBM((owners, snapshots, rows, width), jnp.bfloat16),
        in_specs=[
            hidden_spec,
            pl.BlockSpec((1, owners, share, nodes), lambda s: (s, 0, 0, 0)),
            pl.BlockSpec((1, width, width), lambda s: (layer, 0, 0)),
        ],
        out_specs=pl.BlockSpec((owners, 1, rows, width), lambda s: (0, s, 0, 0)),
        compiler_params=pltpu.CompilerParams(vmem_limit_bytes=VMEM_LIMIT),
        cost_estimate=pl.CostEstimate(
            flops=flops, transcendentals=0, bytes_accessed=snapshots * owners * rows * nodes * 8
        ),
        name=f"structure_{layer}_{start}",
    )(in_hbm(hidden), in_hbm(links), in_hbm(w_struct))


def temporal_kernel(
    first_ref,
    x_ref,
    pos_ref,
    gain_ref,
    wq_hbm,
    wk_hbm,
    wv_hbm,
    wo_hbm,
    wu_hbm,
    wd_hbm,
    out_ref,
    wq,
    wk,
    wv,
    wo,
    wu,
    wd,
    sems,
    mixed,
    rows_sum,
    normed,
    queries,
    key_rows,
    values,
    joined,
    order,
    scores,
    weights,
    *,
    layer,
    first_vertex,
):
    steps, group, width = x_ref.shape
    head_dim = width // HEADS
    pair = 2 * head_dim
    f32 = jnp.float32
    pairs = ((wq_hbm, wq), (wk_hbm, wk), (wv_hbm, wv), (wo_hbm, wo), (wu_hbm, wu), (wd_hbm, wd))
    fetches = [
        pltpu.make_async_copy(source.at[layer], target, sems.at[index])
        for index, (source, target) in enumerate(pairs)
    ]

    row = lax.broadcasted_iota(jnp.int32, (steps, pair), 0)
    lane = lax.broadcasted_iota(jnp.int32, (steps, pair), 1)
    column = lane & (head_dim - 1)
    left = lane < head_dim

    @pl.when(pl.program_id(0) == 0)
    def _():
        for fetch in fetches:
            fetch.start()
        order[...] = jnp.where(row < column, row, jnp.where(row == column, 1 << 20, -1))

    for tile in range(width // LANES):
        mixed[tile] = (
            x_ref[:, :, tile * LANES : (tile + 1) * LANES]
            .astype(f32)
            .reshape(steps * group, LANES)
        )
    gain_one = gain_ref[0, 0:1, :]
    gain_two = gain_ref[0, 1:2, :]
    pos = pos_ref[...].astype(f32)
    for v in range(group):
        span = slice(v * steps, (v + 1) * steps)
        parts = [mixed[tile, pl.ds(v, steps, stride=group), :] for tile in range(width // LANES)]
        total = jnp.concatenate(parts, axis=1) + pos
        rows_sum[span, :] = total
        normed[span, :] = normalise(total, gain_one)

    @pl.when(pl.program_id(0) == 0)
    def _():
        for fetch in fetches[:3]:
            fetch.wait()

    rows = normed[...]
    queries[...] = (jnp.dot(rows, wq[...], preferred_element_type=f32) * head_dim ** (-0.5)).astype(
        jnp.bfloat16
    )
    key_rows[...] = jnp.dot(rows, wk[...], preferred_element_type=f32).astype(jnp.bfloat16)
    values[...] = jnp.dot(rows, wv[...], preferred_element_type=f32).astype(jnp.bfloat16)

    base = first_vertex + pl.program_id(0) * group
    zero = jnp.zeros((steps, pair), jnp.bfloat16)
    for v in range(group):
        span = slice(v * steps, (v + 1) * steps)
        for p in range(width // pair):
            lanes = slice(p * pair, (p + 1) * pair)
            q = queries[span, lanes]
            stacked = jnp.concatenate([jnp.where(left, q, zero), jnp.where(left, zero, q)], axis=0)
            scores[span, lanes] = lax.dot_general(
                key_rows[span, lanes], stacked, (((1,), (1,)), ((), ())), preferred_element_type=f32
            )
    for v in range(group):
        allowed = order[...] >= first_ref[base + v]
        span = slice(v * steps, (v + 1) * steps)
        for p in range(width // pair):
            lanes = slice(p * pair, (p + 1) * pair)
            seen = jnp.where(allowed, scores[span, lanes], -1e30)
            raised = jnp.exp(seen - jnp.max(seen, axis=0, keepdims=True))
            share = 1.0 / jnp.sum(raised, axis=0, keepdims=True)
            weights[span, lanes] = (raised * share).astype(jnp.bfloat16)
    for v in range(group):
        span = slice(v * steps, (v + 1) * steps)
        for p in range(width // pair):
            lanes = slice(p * pair, (p + 1) * pair)
            both = lax.dot_general(
                weights[span, lanes],
                values[span, lanes],
                (((0,), (0,)), ((), ())),
                preferred_element_type=f32,
            )
            joined[span, lanes] = jnp.where(left, both[:steps], both[steps:]).astype(jnp.bfloat16)

    @pl.when(pl.program_id(0) == 0)
    def _():
        for fetch in fetches[3:]:
            fetch.wait()

    attended = rows_sum[...] + jnp.dot(joined[...], wo[...], preferred_element_type=f32)
    inner = jax.nn.gelu(
        jnp.dot(normalise(attended, gain_two), wu[...], preferred_element_type=f32)
    ).astype(jnp.bfloat16)
    finished = attended + jnp.dot(inner, wd[...], preferred_element_type=f32)
    for tile in range(width // LANES):
        lanes = slice(tile * LANES, (tile + 1) * LANES)
        for v in range(group):
            mixed[tile, pl.ds(v, steps, stride=group), :] = finished[
                v * steps : (v + 1) * steps, lanes
            ]
        out_ref[:, :, lanes] = mixed[tile].reshape(steps, group, LANES).astype(jnp.bfloat16)


def temporal_piece(
    rows, first_seen, pos_embed, weights, norm_gain, layer, start, out_count, previous
):
    steps, count, width = rows.shape
    group = min(GROUP, count)
    inner = weights[-1].shape[1]
    size = steps * group
    flops = 2 * steps * count * width * (4 * width + 2 * inner)
    hbm = pl.BlockSpec(memory_space=pltpu.HBM)
    kernel = functools.partial(temporal_kernel, layer=layer, first_vertex=start)
    operands = [first_seen, rows, pos_embed, norm_gain] + [in_hbm(w) for w in weights]
    in_specs = [
        pl.BlockSpec(memory_space=pltpu.SMEM),
        pl.BlockSpec((steps, group, width), lambda i: (0, i, 0)),
        pl.BlockSpec(pos_embed.shape, lambda i: (0, 0)),
        pl.BlockSpec((1,) + norm_gain.shape[1:], lambda i: (layer, 0, 0)),
    ] + [hbm] * len(weights)
    aliases = {}
    if previous is not None:
        aliases = {len(operands): 0}
        operands.append(previous)
        in_specs.append(hbm)
        inner_kernel = kernel

        def kernel(*refs):
            inner_kernel(*refs[: len(operands) - 1], *refs[len(operands) :])

    bf16 = jnp.bfloat16
    return pl.pallas_call(
        kernel,
        grid=(count // group,),
        out_shape=pltpu.HBM((steps, out_count, width), bf16),
        in_specs=in_specs,
        out_specs=pl.BlockSpec((steps, group, width), lambda i: (0, start // group + i, 0)),
        scratch_shapes=[pltpu.VMEM(w.shape[1:], bf16) for w in weights]
        + [
            pltpu.SemaphoreType.DMA((len(weights),)),
            pltpu.VMEM((width // LANES, size, LANES), jnp.float32),
            pltpu.VMEM((size, width), jnp.float32),
            pltpu.VMEM((size, width), bf16),
            pltpu.VMEM((size, width), bf16),
            pltpu.VMEM((size, width), bf16),
            pltpu.VMEM((size, width), bf16),
            pltpu.VMEM((size, width), bf16),
            pltpu.VMEM((steps, 2 * width // HEADS), jnp.int32),
            pltpu.VMEM((size, width), jnp.float32),
            pltpu.VMEM((size, width), bf16),
        ],
        input_output_aliases=aliases,
        compiler_params=pltpu.CompilerParams(vmem_limit_bytes=VMEM_LIMIT),
        cost_estimate=pl.CostEstimate(
            flops=flops, transcendentals=0, bytes_accessed=4 * steps * count * width + 4 * 2**20
        ),
        name=f"temporal_{layer}_{start}",
    )(*operands)


def temporal(x, first_seen, pos_embed, wq, wk, wv, wo, wu, wd, norm_gain, layer, chunk):
    return temporal_piece(
        x, first_seen, pos_embed, (wq, wk, wv, wo, wu, wd), norm_gain, layer, 0, x.shape[1], None
    )


def on_device(
    features,
    adjacency,
    first_seen,
    pos_embed,
    w_struct,
    w_query,
    w_key,
    w_value,
    w_out,
    w_up,
    w_down,
    norm_gain,
    *,
    owners,
):
    snapshots, nodes, width = features.shape
    share = nodes // owners
    lead = share * LEAD_QUARTERS // 4
    chunks = ((0, lead), (lead, share - lead)) if lead < share else ((0, share),)
    weights = (w_query, w_key, w_value, w_out, w_up, w_down)

    def exchange(array):
        return lax.all_to_all(array, "snap", split_axis=0, concat_axis=0, tiled=True)

    hidden = features
    for layer in range(BLOCKS):
        arrived = [
            exchange(structure(hidden, adjacency, w_struct, layer, start, rows, owners))
            for start, rows in chunks
        ]
        finished = None
        for (start, rows), piece in zip(chunks, arrived):
            finished = temporal_piece(
                piece.reshape(owners * snapshots, rows, width),
                first_seen,
                pos_embed,
                weights,
                norm_gain,
                layer,
                start,
                share,
                finished,
            )
        hidden = exchange(finished.reshape(owners, snapshots, share, width))
    return hidden.transpose(1, 0, 2, 3).reshape(snapshots, nodes, width)


def solution(mesh):
    in_specs = (
        P("snap", "clus", None),
        P("snap", "clus", None),
        P(("clus", "snap")),
        P(),
        P(),
        P(),
        P(),
        P(),
        P(),
        P(),
        P(),
        P(),
    )
    out_specs = P("snap", "clus", None)
    return jax.shard_map(
        functools.partial(on_device, owners=mesh.shape["snap"]),
        mesh=mesh,
        in_specs=in_specs,
        out_specs=out_specs,
        check_vma=False,
    )
```

```python
import functools

import jax
import jax.numpy as jnp
from jax import lax
from jax.experimental import pallas as pl
from jax.experimental.pallas import tpu as pltpu
from jax.sharding import PartitionSpec as P

HEADS = 8
BLOCKS = 2
PARTS = 1
SPLIT = 1
OUTWARD = (16, 16)
HOMEWARD = (16, 16)
LANES = 128
VMEM_LIMIT = 32 * 1024 * 1024


def in_hbm(array):
    return pltpu.with_memory_space_constraint(array, pltpu.HBM)


def normalise(rows, gain):
    average = jnp.mean(rows, axis=-1, keepdims=True)
    centred = rows - average
    spread = jnp.mean(centred * centred, axis=-1, keepdims=True)
    return (centred * lax.rsqrt(spread + 1e-05) * gain).astype(jnp.bfloat16)


def bend(mapped):
    return jnp.where(mapped > 0, mapped, jnp.exp(jnp.minimum(mapped, 0.0)) - 1.0)


def structure_kernel(*refs, pieces, layer, start):
    hidden_hbm = refs[:pieces]
    links_hbm, weight_hbm, out_hbm, hidden_buf, links_buf, weight, out_buf, sems = refs[pieces:]
    snapshots, owners, rows, width = out_buf.shape
    nodes = links_buf.shape[-1]
    share = nodes // owners
    loads = []
    for s in range(snapshots):
        group = []
        below = 0
        for index, ref in enumerate(hidden_hbm):
            count = share if ref.ndim == 3 else ref.shape[2]
            if ref.ndim == 3:
                source, target = ref.at[s], hidden_buf.at[s]
            else:
                source, target = ref.at[:, s], hidden_buf.at[s, :, below : below + count]
            group.append(pltpu.make_async_copy(source, target, sems.at[s, index]))
            below += count
        group.append(
            pltpu.make_async_copy(
                links_hbm.at[s, :, start : start + rows], links_buf.at[s], sems.at[s, pieces]
            )
        )
        loads.append(group)
    fetch = pltpu.make_async_copy(weight_hbm.at[layer], weight, sems.at[snapshots, 0])
    for index, group in enumerate(loads):
        for load in group:
            load.start()
        if index == 0:
            fetch.start()
    stores = []
    for s in range(snapshots):
        for load in loads[s]:
            load.wait()
        if s == 0:
            fetch.wait()
        hidden = hidden_buf[s].reshape(nodes, width)
        per = owners // SPLIT
        for part in range(SPLIT):
            span = slice(part * per, (part + 1) * per)
            if hidden_buf.ndim == 3:
                own = hidden_buf[s, part * per * share : (part + 1) * per * share, :]
                own = own.reshape(per, share, width)[:, start : start + rows]
            else:
                own = hidden_buf[s, span, start : start + rows, :]
            own = own.reshape(per * rows, width).astype(jnp.float32)
            links = links_buf[s, span].reshape(per * rows, nodes).astype(jnp.float32)
            scale = 1.0 / (1.0 + jnp.sum(links, axis=1, keepdims=True))
            summed = jnp.dot(
                links.astype(jnp.bfloat16), hidden, preferred_element_type=jnp.float32
            )
            mixture = ((summed + own) * scale).astype(jnp.bfloat16)
            mapped = jnp.dot(mixture, weight[...], preferred_element_type=jnp.float32)
            out_buf[s, span] = (bend(mapped) + own).astype(jnp.bfloat16).reshape(per, rows, width)
        stores.append(
            pltpu.make_async_copy(out_buf.at[s], out_hbm.at[:, s], sems.at[snapshots, s + 1])
        )
        stores[-1].start()
    for store in stores:
        store.wait()


def structure(hidden, adjacency, w_struct, layer, start, rows, owners):
    hidden = hidden if isinstance(hidden, (list, tuple)) else [hidden]
    snapshots, nodes, _ = adjacency.shape
    width = w_struct.shape[-1]
    share = nodes // owners
    links = adjacency.reshape(snapshots, owners, share, nodes)
    near = [in_hbm(h) if h.ndim == 3 else h for h in hidden]
    flops = 2 * snapshots * owners * rows * width * (nodes + width)
    far = pl.BlockSpec(memory_space=pltpu.HBM)
    if hidden[0].ndim == 3:
        hidden_shape = (snapshots, nodes, width)
    else:
        hidden_shape = (snapshots, owners, share, width)
    return pl.pallas_call(
        functools.partial(structure_kernel, pieces=len(hidden), layer=layer, start=start),
        out_shape=pltpu.HBM((owners, snapshots, rows, width), jnp.bfloat16),
        in_specs=[pl.BlockSpec(memory_space=pl.ANY)] * len(hidden) + [far] * 2,
        out_specs=far,
        scratch_shapes=[
            pltpu.VMEM(hidden_shape, jnp.bfloat16),
            pltpu.VMEM((snapshots, owners, rows, nodes), adjacency.dtype),
            pltpu.VMEM((width, width), jnp.bfloat16),
            pltpu.VMEM((snapshots, owners, rows, width), jnp.bfloat16),
            pltpu.SemaphoreType.DMA((snapshots + 1, snapshots + 1)),
        ],
        compiler_params=pltpu.CompilerParams(vmem_limit_bytes=VMEM_LIMIT),
        cost_estimate=pl.CostEstimate(
            flops=flops, transcendentals=0, bytes_accessed=snapshots * nodes * nodes * 8
        ),
        name=f"structure_{layer}_{start}",
    )(*near, in_hbm(links), in_hbm(w_struct))


def temporal_kernel(
    first_ref,
    x_ref,
    pos_ref,
    gain_ref,
    wq_hbm,
    wk_hbm,
    wv_hbm,
    wo_hbm,
    wu_hbm,
    wd_hbm,
    out_ref,
    wq,
    wk,
    wv,
    wo,
    wu,
    wd,
    sems,
    mixed,
    rows_sum,
    normed,
    queries,
    key_rows,
    values,
    joined,
    order,
    scores,
    weights,
    inner,
    *,
    layer,
    offset,
    first_vertex,
):
    steps, group, width = out_ref.shape
    head_dim = width // HEADS
    pair = 2 * head_dim
    f32 = jnp.float32
    pairs = ((wq_hbm, wq), (wk_hbm, wk), (wv_hbm, wv), (wo_hbm, wo), (wu_hbm, wu), (wd_hbm, wd))
    fetches = [
        pltpu.make_async_copy(source.at[layer], target, sems.at[index])
        for index, (source, target) in enumerate(pairs)
    ]

    @pl.when(pl.program_id(0) == 0)
    def _():
        for fetch in fetches:
            fetch.start()

    row = lax.broadcasted_iota(jnp.int32, (steps, pair), 0)
    lane = lax.broadcasted_iota(jnp.int32, (steps, pair), 1)
    column = lane & (head_dim - 1)
    left = lane < head_dim
    order[...] = jnp.where(row < column, row, jnp.where(row == column, 1 << 20, -1))

    gain_one = gain_ref[layer, 0:1, :]
    gain_two = gain_ref[layer, 1:2, :]
    base = first_vertex + pl.program_id(0) * group
    zero = jnp.zeros((steps, pair), jnp.bfloat16)
    tiles = range(width // LANES)
    half = group // PARTS
    first_row = offset + pl.program_id(0) * group

    def enter(part):
        for tile in tiles:
            mixed[part, tile] = (
                x_ref[
                    :,
                    pl.ds(pl.multiple_of(first_row + part * half, half), half),
                    tile * LANES : (tile + 1) * LANES,
                ]
                .astype(f32)
                .reshape(steps * half, LANES)
            )
        pos = pos_ref[...].astype(f32)
        for v in range(half):
            span = slice(v * steps, (v + 1) * steps)
            parts = [mixed[part, tile, pl.ds(v, steps, stride=half), :] for tile in tiles]
            total = jnp.concatenate(parts, axis=1) + pos
            rows_sum[part, span, :] = total
            normed[part, span, :] = normalise(total, gain_one)

    def project(part):
        rows = normed[part]
        queries[part] = (
            jnp.dot(rows, wq[...], preferred_element_type=f32) * head_dim ** (-0.5)
        ).astype(jnp.bfloat16)
        key_rows[part] = jnp.dot(rows, wk[...], preferred_element_type=f32).astype(jnp.bfloat16)
        values[part] = jnp.dot(rows, wv[...], preferred_element_type=f32).astype(jnp.bfloat16)

    def score(part):
        for v in range(half):
            span = slice(v * steps, (v + 1) * steps)
            for p in range(width // pair):
                lanes = slice(p * pair, (p + 1) * pair)
                q = queries[part, span, lanes]
                stacked = jnp.concatenate(
                    [jnp.where(left, q, zero), jnp.where(left, zero, q)], axis=0
                )
                scores[part, span, lanes] = lax.dot_general(
                    key_rows[part, span, lanes],
                    stacked,
                    (((1,), (1,)), ((), ())),
                    preferred_element_type=f32,
                )

    def soften(part):
        for v in range(half):
            allowed = order[...] >= first_ref[base + part * half + v]
            span = slice(v * steps, (v + 1) * steps)
            for p in range(width // pair):
                lanes = slice(p * pair, (p + 1) * pair)
                seen = jnp.where(allowed, scores[part, span, lanes], -1e30)
                raised = jnp.exp(seen - jnp.max(seen, axis=0, keepdims=True))
                share = 1.0 / jnp.sum(raised, axis=0, keepdims=True)
                weights[part, span, lanes] = (raised * share).astype(jnp.bfloat16)

    def gather(part):
        for v in range(half):
            span = slice(v * steps, (v + 1) * steps)
            for p in range(width // pair):
                lanes = slice(p * pair, (p + 1) * pair)
                both = lax.dot_general(
                    weights[part, span, lanes],
                    values[part, span, lanes],
                    (((0,), (0,)), ((), ())),
                    preferred_element_type=f32,
                )
                joined[part, span, lanes] = jnp.where(left, both[:steps], both[steps:]).astype(
                    jnp.bfloat16
                )

    def attend(part):
        attended = rows_sum[part] + jnp.dot(joined[part], wo[...], preferred_element_type=f32)
        rows_sum[part] = attended

    def second_norm(part):
        normed[part] = normalise(rows_sum[part], gain_two)

    def widen(part):
        inner[part] = jax.nn.gelu(
            jnp.dot(normed[part], wu[...], preferred_element_type=f32)
        ).astype(jnp.bfloat16)

    def finish(part):
        finished = rows_sum[part] + jnp.dot(inner[part], wd[...], preferred_element_type=f32)
        for tile in tiles:
            lanes = slice(tile * LANES, (tile + 1) * LANES)
            for v in range(half):
                mixed[part, tile, pl.ds(v, steps, stride=half), :] = finished[
                    v * steps : (v + 1) * steps, lanes
                ]
            out_ref[:, part * half : (part + 1) * half, lanes] = (
                mixed[part, tile].reshape(steps, half, LANES).astype(jnp.bfloat16)
            )

    def wait_for(some):
        @pl.when(pl.program_id(0) == 0)
        def _():
            for fetch in some:
                fetch.wait()

    def run(*stages):
        for stage in stages:
            for part in range(PARTS):
                stage(part)

    run(enter)
    wait_for(fetches[:3])
    run(project, score, soften, gather)
    wait_for(fetches[3:])
    run(attend, second_norm, widen, finish)


def temporal(rows, first_seen, pos_embed, weights, norm_gain, layer, offset, start, count):
    steps, _, width = rows.shape
    group = 8 * PARTS
    inner = weights[4].shape[-1]
    size = 8 * steps
    flops = 2 * steps * count * width * (4 * width + 2 * inner)
    near = pl.BlockSpec(memory_space=pltpu.VMEM)
    bf16 = jnp.bfloat16
    return pl.pallas_call(
        functools.partial(temporal_kernel, layer=layer, offset=offset, first_vertex=start),
        grid=(count // group,),
        out_shape=pltpu.HBM((steps, count, width), bf16),
        in_specs=[pl.BlockSpec(memory_space=pltpu.SMEM)]
        + [near] * 3
        + [pl.BlockSpec(memory_space=pltpu.HBM)] * len(weights),
        out_specs=pl.BlockSpec((steps, group, width), lambda i: (0, i, 0)),
        scratch_shapes=[pltpu.VMEM(w.shape[1:], bf16) for w in weights]
        + [
            pltpu.SemaphoreType.DMA((len(weights),)),
            pltpu.VMEM((PARTS, width // LANES, size, LANES), jnp.float32),
            pltpu.VMEM((PARTS, size, width), jnp.float32),
            pltpu.VMEM((PARTS, size, width), bf16),
            pltpu.VMEM((PARTS, size, width), bf16),
            pltpu.VMEM((PARTS, size, width), bf16),
            pltpu.VMEM((PARTS, size, width), bf16),
            pltpu.VMEM((PARTS, size, width), bf16),
            pltpu.VMEM((steps, 2 * width // HEADS), jnp.int32),
            pltpu.VMEM((PARTS, size, width), jnp.float32),
            pltpu.VMEM((PARTS, size, width), bf16),
            pltpu.VMEM((PARTS, size, inner), bf16),
        ],
        compiler_params=pltpu.CompilerParams(vmem_limit_bytes=VMEM_LIMIT),
        cost_estimate=pl.CostEstimate(
            flops=flops, transcendentals=0, bytes_accessed=2 * steps * count * width
        ),
        name=f"temporal_{layer}_{start}",
    )(first_seen, rows, pos_embed, norm_gain, *[in_hbm(w) for w in weights])


def deliver_kernel(piece_ref, *refs, start):
    out_hbm, sems = refs[-2:]
    owners, snapshots, rows, _ = piece_ref.shape
    stores = [
        pltpu.make_async_copy(
            piece_ref.at[:, s], out_hbm.at[s, :, start : start + rows], sems.at[s]
        )
        for s in range(snapshots)
    ]
    for store in stores:
        store.start()
    for store in stores:
        store.wait()


def deliver(piece, target, start, share):
    owners, snapshots, _, width = piece.shape
    far = pl.BlockSpec(memory_space=pltpu.HBM)
    operands = [piece] if target is None else [piece, target]
    return pl.pallas_call(
        functools.partial(deliver_kernel, start=start),
        out_shape=pltpu.HBM((snapshots, owners, share, width), piece.dtype),
        in_specs=[pl.BlockSpec(memory_space=pltpu.VMEM)] + [far] * (len(operands) - 1),
        out_specs=far,
        scratch_shapes=[pltpu.SemaphoreType.DMA((snapshots,))],
        input_output_aliases={} if target is None else {1: 0},
        compiler_params=pltpu.CompilerParams(vmem_limit_bytes=VMEM_LIMIT),
        cost_estimate=pl.CostEstimate(
            flops=0, transcendentals=0, bytes_accessed=2 * piece.size * 2
        ),
        name=f"deliver_{start}",
    )(*operands)


def on_device(
    features,
    adjacency,
    first_seen,
    pos_embed,
    w_struct,
    w_query,
    w_key,
    w_value,
    w_out,
    w_up,
    w_down,
    norm_gain,
    *,
    owners,
):
    snapshots, nodes, width = features.shape

    def exchange(array):
        return lax.all_to_all(array, "snap", split_axis=0, concat_axis=0, tiled=True)

    weights = (w_query, w_key, w_value, w_out, w_up, w_down)
    hidden = [features]
    for layer in range(BLOCKS):
        arrived = []
        start = 0
        for rows in OUTWARD:
            piece = structure(hidden, adjacency, w_struct, layer, start, rows, owners)
            piece = exchange(piece)
            arrived.append((start, piece.reshape(owners * snapshots, rows, width)))
            start += rows
        hidden = []
        start = 0
        for rows in HOMEWARD:
            at, piece = [item for item in arrived if item[0] <= start][-1]
            finished = temporal(
                piece, first_seen, pos_embed, weights, norm_gain, layer, start - at, start, rows
            )
            hidden.append(exchange(finished.reshape(owners, snapshots, rows, width)))
            start += rows
    result = None
    start = 0
    for piece in hidden:
        result = deliver(piece, result, start, nodes // owners)
        start += piece.shape[2]
    return result.reshape(snapshots, nodes, width)


def solution(mesh):
    in_specs = (
        P("snap", "clus", None),
        P("snap", "clus", None),
        P(("clus", "snap")),
        P(),
        P(),
        P(),
        P(),
        P(),
        P(),
        P(),
        P(),
        P(),
    )
    out_specs = P("snap", "clus", None)
    return jax.shard_map(
        functools.partial(on_device, owners=mesh.shape["snap"]),
        mesh=mesh,
        in_specs=in_specs,
        out_specs=out_specs,
        check_vma=False,
    )
```

```python
import functools

import jax
import jax.numpy as jnp
from jax import lax
from jax.experimental import pallas as pl
from jax.experimental.pallas import tpu as pltpu
from jax.sharding import PartitionSpec as P

HEADS = 8
BLOCKS = 2
PARTS = 1
OUTWARD = (16, 16)
HOMEWARD = (16, 16)
LANES = 128
VMEM_LIMIT = 32 * 1024 * 1024


def in_hbm(array):
    return pltpu.with_memory_space_constraint(array, pltpu.HBM)


def normalise(rows, gain):
    average = jnp.mean(rows, axis=-1, keepdims=True)
    centred = rows - average
    spread = jnp.mean(centred * centred, axis=-1, keepdims=True)
    return (centred * lax.rsqrt(spread + 1e-05) * gain).astype(jnp.bfloat16)


def bend(mapped):
    return jnp.where(mapped > 0, mapped, jnp.exp(jnp.minimum(mapped, 0.0)) - 1.0)


def structure_kernel(*refs, pieces, layer, start):
    hidden_hbm = refs[:pieces]
    links_hbm, weight_hbm, out_hbm, hidden_buf, links_buf, weight, out_buf, *rest = refs[pieces:]
    scales, narrow, mixture, sems = rest
    snapshots, owners, rows, width = out_buf.shape
    nodes = links_buf.shape[-1]
    share = nodes // owners
    loads = []
    for s in range(snapshots):
        group = []
        below = 0
        for index, ref in enumerate(hidden_hbm):
            count = share if ref.ndim == 3 else ref.shape[2]
            if ref.ndim == 3:
                source, target = ref.at[s], hidden_buf.at[s]
            else:
                source, target = ref.at[:, s], hidden_buf.at[s, :, below : below + count]
            group.append(pltpu.make_async_copy(source, target, sems.at[s, index]))
            below += count
        group.append(
            pltpu.make_async_copy(
                links_hbm.at[s, :, start : start + rows], links_buf.at[s], sems.at[s, pieces]
            )
        )
        loads.append(group)
    fetch = pltpu.make_async_copy(weight_hbm.at[layer], weight, sems.at[snapshots, 0])
    for index, group in enumerate(loads):
        for load in group:
            load.start()
        if index == 0:
            fetch.start()
    stores = []

    def own_rows(s):
        if hidden_buf.ndim == 3:
            own = hidden_buf[s].reshape(owners, share, width)[:, start : start + rows]
        else:
            own = hidden_buf[s, :, start : start + rows, :]
        return own.reshape(owners * rows, width).astype(jnp.float32)

    def ready(s):
        for load in loads[s]:
            load.wait()
        if s == 0:
            fetch.wait()
        links = links_buf[s].reshape(owners * rows, nodes).astype(jnp.float32)
        scale = 1.0 / (1.0 + jnp.sum(links, axis=1, keepdims=True))
        scales[s] = jnp.broadcast_to(scale, (owners * rows, LANES))
        narrow[s] = links.astype(jnp.bfloat16)

    def mix(s):
        summed = jnp.dot(
            narrow[s], hidden_buf[s].reshape(nodes, width), preferred_element_type=jnp.float32
        )
        scale = jnp.concatenate([scales[s]] * (width // LANES), axis=1)
        mixture[s] = ((summed + own_rows(s)) * scale).astype(jnp.bfloat16)

    def settle(s):
        mapped = jnp.dot(mixture[s], weight[...], preferred_element_type=jnp.float32)
        rounded = (bend(mapped) + own_rows(s)).astype(jnp.bfloat16)
        out_buf[s] = rounded.reshape(owners, rows, width)
        stores.append(
            pltpu.make_async_copy(out_buf.at[s], out_hbm.at[:, s], sems.at[snapshots, s + 1])
        )
        stores[-1].start()

    stages = (ready, mix, settle)
    for tick in range(snapshots + len(stages) - 1):
        for lag, step in enumerate(stages):
            if 0 <= tick - lag < snapshots:
                step(tick - lag)
    for store in stores:
        store.wait()


def structure(hidden, adjacency, w_struct, layer, start, rows, owners):
    hidden = hidden if isinstance(hidden, (list, tuple)) else [hidden]
    snapshots, nodes, _ = adjacency.shape
    width = w_struct.shape[-1]
    share = nodes // owners
    links = adjacency.reshape(snapshots, owners, share, nodes)
    near = [in_hbm(h) if h.ndim == 3 else h for h in hidden]
    flops = 2 * snapshots * owners * rows * width * (nodes + width)
    far = pl.BlockSpec(memory_space=pltpu.HBM)
    if hidden[0].ndim == 3:
        hidden_shape = (snapshots, nodes, width)
    else:
        hidden_shape = (snapshots, owners, share, width)
    return pl.pallas_call(
        functools.partial(structure_kernel, pieces=len(hidden), layer=layer, start=start),
        out_shape=pltpu.HBM((owners, snapshots, rows, width), jnp.bfloat16),
        in_specs=[pl.BlockSpec(memory_space=pl.ANY)] * len(hidden) + [far] * 2,
        out_specs=far,
        scratch_shapes=[
            pltpu.VMEM(hidden_shape, jnp.bfloat16),
            pltpu.VMEM((snapshots, owners, rows, nodes), adjacency.dtype),
            pltpu.VMEM((width, width), jnp.bfloat16),
            pltpu.VMEM((snapshots, owners, rows, width), jnp.bfloat16),
            pltpu.VMEM((snapshots, owners * rows, LANES), jnp.float32),
            pltpu.VMEM((snapshots, owners * rows, nodes), jnp.bfloat16),
            pltpu.VMEM((snapshots, owners * rows, width), jnp.bfloat16),
            pltpu.SemaphoreType.DMA((snapshots + 1, snapshots + 1)),
        ],
        compiler_params=pltpu.CompilerParams(vmem_limit_bytes=VMEM_LIMIT),
        cost_estimate=pl.CostEstimate(
            flops=flops, transcendentals=0, bytes_accessed=snapshots * nodes * nodes * 8
        ),
        name=f"structure_{layer}_{start}",
    )(*near, in_hbm(links), in_hbm(w_struct))


def stage_kernel(links_hbm, after_hbm, narrow_hbm, scale_ref, whole, narrow, sems):
    del after_hbm
    snapshots, nodes, _ = whole.shape
    loads = [
        pltpu.make_async_copy(links_hbm.at[s], whole.at[s], sems.at[0, s]) for s in range(snapshots)
    ]
    stores = [
        pltpu.make_async_copy(narrow.at[s], narrow_hbm.at[s], sems.at[1, s])
        for s in range(snapshots)
    ]
    for load in loads:
        load.start()
    for s in range(snapshots):
        loads[s].wait()
        links = whole[s].astype(jnp.float32)
        scale = 1.0 / (1.0 + jnp.sum(links, axis=1, keepdims=True))
        scale_ref[s] = jnp.broadcast_to(scale, (nodes, LANES))
        narrow[s] = links.astype(jnp.bfloat16)
        stores[s].start()
    for store in stores:
        store.wait()


def stage(adjacency, after):
    snapshots, nodes, _ = adjacency.shape
    far = pl.BlockSpec(memory_space=pltpu.HBM)
    return pl.pallas_call(
        stage_kernel,
        out_shape=[
            pltpu.HBM(adjacency.shape, jnp.bfloat16),
            pltpu.VMEM((snapshots, nodes, LANES), jnp.float32),
        ],
        in_specs=[far] * 2,
        out_specs=[far, pl.BlockSpec(memory_space=pltpu.VMEM)],
        scratch_shapes=[
            pltpu.VMEM(adjacency.shape, adjacency.dtype),
            pltpu.VMEM(adjacency.shape, jnp.bfloat16),
            pltpu.SemaphoreType.DMA((2, snapshots)),
        ],
        compiler_params=pltpu.CompilerParams(vmem_limit_bytes=VMEM_LIMIT),
        cost_estimate=pl.CostEstimate(
            flops=0, transcendentals=0, bytes_accessed=adjacency.size * 6 + 2**20
        ),
        name="stage",
    )(in_hbm(adjacency), in_hbm(after))


def restructure_kernel(*refs, pieces, layer, start):
    hidden_refs = refs[:pieces]
    links_hbm, scale_ref, weight_hbm, out_hbm = refs[pieces : pieces + 4]
    links_buf, weight, gathered, mixture, out_buf, sems = refs[pieces + 4 :]
    snapshots, owners, rows, width = out_buf.shape
    nodes = links_hbm.shape[-1]
    share = nodes // owners
    chosen = slice(start, start + rows)
    loads = [
        pltpu.make_async_copy(links_hbm.at[s, :, chosen], links_buf.at[s], sems.at[0, s])
        for s in range(snapshots)
    ]
    fetch = pltpu.make_async_copy(weight_hbm.at[layer], weight, sems.at[0, snapshots])
    loads[0].start()
    fetch.start()
    for load in loads[1:]:
        load.start()

    def ready(s):
        below = 0
        for ref in hidden_refs:
            count = ref.shape[2]
            gathered[s, :, below : below + count, :] = ref[:, s]
            below += count

    def own_rows(s):
        return gathered[s, :, chosen, :].reshape(owners * rows, width).astype(jnp.float32)

    def mix(s):
        loads[s].wait()
        links = links_buf[s].reshape(owners * rows, nodes)
        scale = scale_ref[s].reshape(owners, share, LANES)[:, chosen].reshape(owners * rows, LANES)
        scale = jnp.concatenate([scale] * (width // LANES), axis=1)
        summed = jnp.dot(
            links, gathered[s].reshape(nodes, width), preferred_element_type=jnp.float32
        )
        mixture[s] = ((summed + own_rows(s)) * scale).astype(jnp.bfloat16)

    stores = []

    def settle(s):
        if s == 0:
            fetch.wait()
        mapped = jnp.dot(mixture[s], weight[...], preferred_element_type=jnp.float32)
        rounded = (bend(mapped) + own_rows(s)).astype(jnp.bfloat16)
        out_buf[s] = rounded.reshape(owners, rows, width)
        stores.append(pltpu.make_async_copy(out_buf.at[s], out_hbm.at[:, s], sems.at[1, s]))
        stores[-1].start()

    stages = (ready, mix, settle)
    for tick in range(snapshots + len(stages) - 1):
        for lag, step in enumerate(stages):
            if 0 <= tick - lag < snapshots:
                step(tick - lag)
    for store in stores:
        store.wait()


def restructure(hidden, links, scale, w_struct, layer, start, rows):
    snapshots, nodes, _ = links.shape
    width = w_struct.shape[-1]
    owners = hidden[0].shape[0]
    share = nodes // owners
    flops = 2 * snapshots * owners * rows * width * (nodes + width)
    near = pl.BlockSpec(memory_space=pltpu.VMEM)
    far = pl.BlockSpec(memory_space=pltpu.HBM)
    return pl.pallas_call(
        functools.partial(restructure_kernel, pieces=len(hidden), layer=layer, start=start),
        out_shape=pltpu.HBM((owners, snapshots, rows, width), jnp.bfloat16),
        in_specs=[near] * len(hidden) + [far, near, far],
        out_specs=far,
        scratch_shapes=[
            pltpu.VMEM((snapshots, owners, rows, nodes), jnp.bfloat16),
            pltpu.VMEM((width, width), jnp.bfloat16),
            pltpu.VMEM((snapshots, owners, share, width), jnp.bfloat16),
            pltpu.VMEM((snapshots, owners * rows, width), jnp.bfloat16),
            pltpu.VMEM((snapshots, owners, rows, width), jnp.bfloat16),
            pltpu.SemaphoreType.DMA((2, snapshots + 1)),
        ],
        compiler_params=pltpu.CompilerParams(vmem_limit_bytes=VMEM_LIMIT),
        cost_estimate=pl.CostEstimate(
            flops=flops, transcendentals=0, bytes_accessed=snapshots * owners * rows * width * 6
        ),
        name=f"structure_{layer}_{start}",
    )(*hidden, in_hbm(links.reshape(snapshots, owners, share, nodes)), scale, in_hbm(w_struct))


def temporal_kernel(
    first_ref,
    x_ref,
    pos_ref,
    gain_ref,
    wq_hbm,
    wk_hbm,
    wv_hbm,
    wo_hbm,
    wu_hbm,
    wd_hbm,
    out_ref,
    wq,
    wk,
    wv,
    wo,
    wu,
    wd,
    sems,
    mixed,
    rows_sum,
    normed,
    queries,
    key_rows,
    values,
    joined,
    order,
    scores,
    weights,
    inner,
    *,
    layer,
    offset,
    first_vertex,
):
    steps, group, width = out_ref.shape
    head_dim = width // HEADS
    pair = 2 * head_dim
    f32 = jnp.float32
    pairs = ((wq_hbm, wq), (wk_hbm, wk), (wv_hbm, wv), (wo_hbm, wo), (wu_hbm, wu), (wd_hbm, wd))
    fetches = [
        pltpu.make_async_copy(source.at[layer], target, sems.at[index])
        for index, (source, target) in enumerate(pairs)
    ]

    @pl.when(pl.program_id(0) == 0)
    def _():
        for fetch in fetches:
            fetch.start()

    row = lax.broadcasted_iota(jnp.int32, (steps, pair), 0)
    lane = lax.broadcasted_iota(jnp.int32, (steps, pair), 1)
    column = lane & (head_dim - 1)
    left = lane < head_dim
    order[...] = jnp.where(row < column, row, jnp.where(row == column, 1 << 20, -1))

    gain_one = gain_ref[layer, 0:1, :]
    gain_two = gain_ref[layer, 1:2, :]
    base = first_vertex + pl.program_id(0) * group
    zero = jnp.zeros((steps, pair), jnp.bfloat16)
    tiles = range(width // LANES)
    half = group // PARTS
    first_row = offset + pl.program_id(0) * group

    def enter(part):
        for tile in tiles:
            mixed[part, tile] = (
                x_ref[
                    :,
                    pl.ds(pl.multiple_of(first_row + part * half, half), half),
                    tile * LANES : (tile + 1) * LANES,
                ]
                .astype(f32)
                .reshape(steps * half, LANES)
            )
        pos = pos_ref[...].astype(f32)
        for v in range(half):
            span = slice(v * steps, (v + 1) * steps)
            parts = [mixed[part, tile, pl.ds(v, steps, stride=half), :] for tile in tiles]
            total = jnp.concatenate(parts, axis=1) + pos
            rows_sum[part, span, :] = total
            normed[part, span, :] = normalise(total, gain_one)

    def project(part):
        rows = normed[part]
        queries[part] = (
            jnp.dot(rows, wq[...], preferred_element_type=f32) * head_dim ** (-0.5)
        ).astype(jnp.bfloat16)
        key_rows[part] = jnp.dot(rows, wk[...], preferred_element_type=f32).astype(jnp.bfloat16)
        values[part] = jnp.dot(rows, wv[...], preferred_element_type=f32).astype(jnp.bfloat16)

    def score(part):
        for v in range(half):
            span = slice(v * steps, (v + 1) * steps)
            for p in range(width // pair):
                lanes = slice(p * pair, (p + 1) * pair)
                q = queries[part, span, lanes]
                stacked = jnp.concatenate(
                    [jnp.where(left, q, zero), jnp.where(left, zero, q)], axis=0
                )
                scores[part, span, lanes] = lax.dot_general(
                    key_rows[part, span, lanes],
                    stacked,
                    (((1,), (1,)), ((), ())),
                    preferred_element_type=f32,
                )

    def soften(part):
        for v in range(half):
            allowed = order[...] >= first_ref[base + part * half + v]
            span = slice(v * steps, (v + 1) * steps)
            for p in range(width // pair):
                lanes = slice(p * pair, (p + 1) * pair)
                seen = jnp.where(allowed, scores[part, span, lanes], -1e30)
                raised = jnp.exp(seen - jnp.max(seen, axis=0, keepdims=True))
                share = 1.0 / jnp.sum(raised, axis=0, keepdims=True)
                weights[part, span, lanes] = (raised * share).astype(jnp.bfloat16)

    def gather(part):
        for v in range(half):
            span = slice(v * steps, (v + 1) * steps)
            for p in range(width // pair):
                lanes = slice(p * pair, (p + 1) * pair)
                both = lax.dot_general(
                    weights[part, span, lanes],
                    values[part, span, lanes],
                    (((0,), (0,)), ((), ())),
                    preferred_element_type=f32,
                )
                joined[part, span, lanes] = jnp.where(left, both[:steps], both[steps:]).astype(
                    jnp.bfloat16
                )

    def attend(part):
        attended = rows_sum[part] + jnp.dot(joined[part], wo[...], preferred_element_type=f32)
        rows_sum[part] = attended

    def second_norm(part):
        normed[part] = normalise(rows_sum[part], gain_two)

    def widen(part):
        inner[part] = jax.nn.gelu(
            jnp.dot(normed[part], wu[...], preferred_element_type=f32)
        ).astype(jnp.bfloat16)

    def finish(part):
        finished = rows_sum[part] + jnp.dot(inner[part], wd[...], preferred_element_type=f32)
        for tile in tiles:
            lanes = slice(tile * LANES, (tile + 1) * LANES)
            for v in range(half):
                mixed[part, tile, pl.ds(v, steps, stride=half), :] = finished[
                    v * steps : (v + 1) * steps, lanes
                ]
            out_ref[:, part * half : (part + 1) * half, lanes] = (
                mixed[part, tile].reshape(steps, half, LANES).astype(jnp.bfloat16)
            )

    def wait_for(some):
        @pl.when(pl.program_id(0) == 0)
        def _():
            for fetch in some:
                fetch.wait()

    def run(*stages):
        for stage in stages:
            for part in range(PARTS):
                stage(part)

    run(enter)
    wait_for(fetches[:3])
    run(project, score, soften, gather)
    wait_for(fetches[3:])
    run(attend, second_norm, widen, finish)


def temporal(rows, first_seen, pos_embed, weights, norm_gain, layer, offset, start, count):
    steps, _, width = rows.shape
    group = 8 * PARTS
    inner = weights[4].shape[-1]
    size = 8 * steps
    flops = 2 * steps * count * width * (4 * width + 2 * inner)
    near = pl.BlockSpec(memory_space=pltpu.VMEM)
    bf16 = jnp.bfloat16
    return pl.pallas_call(
        functools.partial(temporal_kernel, layer=layer, offset=offset, first_vertex=start),
        grid=(count // group,),
        out_shape=pltpu.HBM((steps, count, width), bf16),
        in_specs=[pl.BlockSpec(memory_space=pltpu.SMEM)]
        + [near] * 3
        + [pl.BlockSpec(memory_space=pltpu.HBM)] * len(weights),
        out_specs=pl.BlockSpec((steps, group, width), lambda i: (0, i, 0)),
        scratch_shapes=[pltpu.VMEM(w.shape[1:], bf16) for w in weights]
        + [
            pltpu.SemaphoreType.DMA((len(weights),)),
            pltpu.VMEM((PARTS, width // LANES, size, LANES), jnp.float32),
            pltpu.VMEM((PARTS, size, width), jnp.float32),
            pltpu.VMEM((PARTS, size, width), bf16),
            pltpu.VMEM((PARTS, size, width), bf16),
            pltpu.VMEM((PARTS, size, width), bf16),
            pltpu.VMEM((PARTS, size, width), bf16),
            pltpu.VMEM((PARTS, size, width), bf16),
            pltpu.VMEM((steps, 2 * width // HEADS), jnp.int32),
            pltpu.VMEM((PARTS, size, width), jnp.float32),
            pltpu.VMEM((PARTS, size, width), bf16),
            pltpu.VMEM((PARTS, size, inner), bf16),
        ],
        compiler_params=pltpu.CompilerParams(vmem_limit_bytes=VMEM_LIMIT),
        cost_estimate=pl.CostEstimate(
            flops=flops, transcendentals=0, bytes_accessed=2 * steps * count * width
        ),
        name=f"temporal_{layer}_{start}",
    )(first_seen, rows, pos_embed, norm_gain, *[in_hbm(w) for w in weights])


def deliver_kernel(piece_ref, *refs, start):
    out_hbm, sems = refs[-2:]
    owners, snapshots, rows, _ = piece_ref.shape
    stores = [
        pltpu.make_async_copy(
            piece_ref.at[:, s], out_hbm.at[s, :, start : start + rows], sems.at[s]
        )
        for s in range(snapshots)
    ]
    for store in stores:
        store.start()
    for store in stores:
        store.wait()


def deliver(piece, target, start, share):
    owners, snapshots, _, width = piece.shape
    far = pl.BlockSpec(memory_space=pltpu.HBM)
    operands = [piece] if target is None else [piece, target]
    return pl.pallas_call(
        functools.partial(deliver_kernel, start=start),
        out_shape=pltpu.HBM((snapshots, owners, share, width), piece.dtype),
        in_specs=[pl.BlockSpec(memory_space=pltpu.VMEM)] + [far] * (len(operands) - 1),
        out_specs=far,
        scratch_shapes=[pltpu.SemaphoreType.DMA((snapshots,))],
        input_output_aliases={} if target is None else {1: 0},
        compiler_params=pltpu.CompilerParams(vmem_limit_bytes=VMEM_LIMIT),
        cost_estimate=pl.CostEstimate(
            flops=0, transcendentals=0, bytes_accessed=2 * piece.size * 2
        ),
        name=f"deliver_{start}",
    )(*operands)


def on_device(
    features,
    adjacency,
    first_seen,
    pos_embed,
    w_struct,
    w_query,
    w_key,
    w_value,
    w_out,
    w_up,
    w_down,
    norm_gain,
    *,
    owners,
):
    snapshots, nodes, width = features.shape

    def exchange(array):
        return lax.all_to_all(array, "snap", split_axis=0, concat_axis=0, tiled=True)

    weights = (w_query, w_key, w_value, w_out, w_up, w_down)
    hidden = [features]
    for layer in range(BLOCKS):
        arrived = []
        start = 0
        for rows in OUTWARD:
            if layer == 0:
                piece = structure(hidden, adjacency, w_struct, layer, start, rows, owners)
            else:
                piece = restructure(hidden, *staged, w_struct, layer, start, rows)
            piece = exchange(piece)
            arrived.append((start, piece.reshape(owners * snapshots, rows, width)))
            start += rows
        hidden = []
        start = 0
        for rows in HOMEWARD:
            at, piece = [item for item in arrived if item[0] <= start][-1]
            finished = temporal(
                piece, first_seen, pos_embed, weights, norm_gain, layer, start - at, start, rows
            )
            hidden.append(exchange(finished.reshape(owners, snapshots, rows, width)))
            start += rows
        if layer + 1 < BLOCKS:
            staged = stage(adjacency, finished)
    result = None
    start = 0
    for piece in hidden:
        result = deliver(piece, result, start, nodes // owners)
        start += piece.shape[2]
    return result.reshape(snapshots, nodes, width)


def solution(mesh):
    in_specs = (
        P("snap", "clus", None),
        P("snap", "clus", None),
        P(("clus", "snap")),
        P(),
        P(),
        P(),
        P(),
        P(),
        P(),
        P(),
        P(),
        P(),
    )
    out_specs = P("snap", "clus", None)
    return jax.shard_map(
        functools.partial(on_device, owners=mesh.shape["snap"]),
        mesh=mesh,
        in_specs=in_specs,
        out_specs=out_specs,
        check_vma=False,
    )
```

```python
import functools

import jax
import jax.numpy as jnp
from jax import lax
from jax.experimental import pallas as pl
from jax.experimental.pallas import tpu as pltpu
from jax.sharding import PartitionSpec as P

HEADS = 8
BLOCKS = 2
PARTS = 1
OUTWARD = (16, 16)
HOMEWARD = (16, 16)
LANES = 128
VMEM_LIMIT = 32 * 1024 * 1024


def in_hbm(array):
    return pltpu.with_memory_space_constraint(array, pltpu.HBM)


def normalise(rows, gain):
    average = jnp.mean(rows, axis=-1, keepdims=True)
    centred = rows - average
    spread = jnp.mean(centred * centred, axis=-1, keepdims=True)
    return (centred * lax.rsqrt(spread + 1e-05) * gain).astype(jnp.bfloat16)


def bend(mapped):
    return jnp.where(mapped > 0, mapped, jnp.exp(jnp.minimum(mapped, 0.0)) - 1.0)


def structure_kernel(*refs, pieces, layer, start):
    hidden_hbm = refs[:pieces]
    links_hbm, weight_hbm, out_hbm, hidden_buf, links_buf, weight, out_buf, *rest = refs[pieces:]
    scales, narrow, mixture, sems = rest
    snapshots, owners, rows, width = out_buf.shape
    nodes = links_buf.shape[-1]
    share = nodes // owners
    loads = []
    for s in range(snapshots):
        group = []
        below = 0
        for index, ref in enumerate(hidden_hbm):
            count = share if ref.ndim == 3 else ref.shape[2]
            if ref.ndim == 3:
                source, target = ref.at[s], hidden_buf.at[s]
            else:
                source, target = ref.at[:, s], hidden_buf.at[s, :, below : below + count]
            group.append(pltpu.make_async_copy(source, target, sems.at[s, index]))
            below += count
        group.append(
            pltpu.make_async_copy(
                links_hbm.at[s, :, start : start + rows], links_buf.at[s], sems.at[s, pieces]
            )
        )
        loads.append(group)
    fetch = pltpu.make_async_copy(weight_hbm.at[layer], weight, sems.at[snapshots, 0])
    for index, group in enumerate(loads):
        for load in group:
            load.start()
        if index == 0:
            fetch.start()
    stores = []

    def own_rows(s):
        if hidden_buf.ndim == 3:
            own = hidden_buf[s].reshape(owners, share, width)[:, start : start + rows]
        else:
            own = hidden_buf[s, :, start : start + rows, :]
        return own.reshape(owners * rows, width).astype(jnp.float32)

    def ready(s):
        for load in loads[s]:
            load.wait()
        if s == 0:
            fetch.wait()
        links = links_buf[s].reshape(owners * rows, nodes).astype(jnp.float32)
        scale = 1.0 / (1.0 + jnp.sum(links, axis=1, keepdims=True))
        scales[s] = jnp.broadcast_to(scale, (owners * rows, LANES))
        narrow[s] = links.astype(jnp.bfloat16)

    def mix(s):
        summed = jnp.dot(
            narrow[s], hidden_buf[s].reshape(nodes, width), preferred_element_type=jnp.float32
        )
        scale = jnp.concatenate([scales[s]] * (width // LANES), axis=1)
        mixture[s] = ((summed + own_rows(s)) * scale).astype(jnp.bfloat16)

    def settle(s):
        mapped = jnp.dot(mixture[s], weight[...], preferred_element_type=jnp.float32)
        rounded = (bend(mapped) + own_rows(s)).astype(jnp.bfloat16)
        out_buf[s] = rounded.reshape(owners, rows, width)
        stores.append(
            pltpu.make_async_copy(out_buf.at[s], out_hbm.at[:, s], sems.at[snapshots, s + 1])
        )
        stores[-1].start()

    stages = (ready, mix, settle)
    for tick in range(snapshots + len(stages) - 1):
        for lag, step in enumerate(stages):
            if 0 <= tick - lag < snapshots:
                step(tick - lag)
    for store in stores:
        store.wait()


def structure(hidden, adjacency, w_struct, layer, start, rows, owners):
    hidden = hidden if isinstance(hidden, (list, tuple)) else [hidden]
    snapshots, nodes, _ = adjacency.shape
    width = w_struct.shape[-1]
    share = nodes // owners
    links = adjacency.reshape(snapshots, owners, share, nodes)
    near = [in_hbm(h) if h.ndim == 3 else h for h in hidden]
    flops = 2 * snapshots * owners * rows * width * (nodes + width)
    far = pl.BlockSpec(memory_space=pltpu.HBM)
    if hidden[0].ndim == 3:
        hidden_shape = (snapshots, nodes, width)
    else:
        hidden_shape = (snapshots, owners, share, width)
    return pl.pallas_call(
        functools.partial(structure_kernel, pieces=len(hidden), layer=layer, start=start),
        out_shape=pltpu.HBM((owners, snapshots, rows, width), jnp.bfloat16),
        in_specs=[pl.BlockSpec(memory_space=pl.ANY)] * len(hidden) + [far] * 2,
        out_specs=far,
        scratch_shapes=[
            pltpu.VMEM(hidden_shape, jnp.bfloat16),
            pltpu.VMEM((snapshots, owners, rows, nodes), adjacency.dtype),
            pltpu.VMEM((width, width), jnp.bfloat16),
            pltpu.VMEM((snapshots, owners, rows, width), jnp.bfloat16),
            pltpu.VMEM((snapshots, owners * rows, LANES), jnp.float32),
            pltpu.VMEM((snapshots, owners * rows, nodes), jnp.bfloat16),
            pltpu.VMEM((snapshots, owners * rows, width), jnp.bfloat16),
            pltpu.SemaphoreType.DMA((snapshots + 1, snapshots + 1)),
        ],
        compiler_params=pltpu.CompilerParams(vmem_limit_bytes=VMEM_LIMIT),
        cost_estimate=pl.CostEstimate(
            flops=flops, transcendentals=0, bytes_accessed=snapshots * nodes * nodes * 8
        ),
        name=f"structure_{layer}_{start}",
    )(*near, in_hbm(links), in_hbm(w_struct))


def stage_kernel(links_hbm, after_hbm, staged_ref, whole, sems):
    del after_hbm
    snapshots, owners, rows, nodes = whole.shape
    loads = [
        pltpu.make_async_copy(links_hbm.at[s, :, 0:rows], whole.at[s], sems.at[s])
        for s in range(snapshots)
    ]
    for load in loads:
        load.start()
    for s in range(snapshots):
        loads[s].wait()
        links = whole[s].reshape(owners * rows, nodes)
        staged_ref[s] = links.astype(jnp.float32).astype(jnp.bfloat16)


def stage(adjacency, owners, rows, after):
    snapshots, nodes, _ = adjacency.shape
    far = pl.BlockSpec(memory_space=pltpu.HBM)
    links = adjacency.reshape(snapshots, owners, nodes // owners, nodes)
    return pl.pallas_call(
        stage_kernel,
        out_shape=pltpu.VMEM((snapshots, owners * rows, nodes), jnp.bfloat16),
        in_specs=[far] * 2,
        out_specs=pl.BlockSpec(memory_space=pltpu.VMEM),
        scratch_shapes=[
            pltpu.VMEM((snapshots, owners, rows, nodes), adjacency.dtype),
            pltpu.SemaphoreType.DMA((snapshots,)),
        ],
        compiler_params=pltpu.CompilerParams(vmem_limit_bytes=VMEM_LIMIT),
        cost_estimate=pl.CostEstimate(
            flops=0, transcendentals=0, bytes_accessed=adjacency.size * 3
        ),
        name="stage",
    )(in_hbm(links), in_hbm(after))


def restructure_kernel(*refs, pieces, layer, start):
    hidden_refs = refs[:pieces]
    staged_ref, weight_hbm, out_hbm, weight, gathered, scales, mixture, out_buf, sems = refs[pieces:]
    snapshots, owners, rows, width = out_buf.shape
    nodes = staged_ref.shape[-1]
    chosen = slice(start, start + rows)
    fetch = pltpu.make_async_copy(weight_hbm.at[layer], weight, sems.at[snapshots])
    fetch.start()

    def links_of(s):
        return staged_ref[s]

    def ready(s):
        below = 0
        for ref in hidden_refs:
            count = ref.shape[2]
            gathered[s, :, below : below + count, :] = ref[:, s]
            below += count
        degree = 1.0 + jnp.sum(links_of(s).astype(jnp.float32), axis=1, keepdims=True)
        scales[s] = jnp.broadcast_to(1.0 / degree, (owners * rows, LANES))

    def own_rows(s):
        return gathered[s, :, chosen, :].reshape(owners * rows, width).astype(jnp.float32)

    def mix(s):
        scale = jnp.concatenate([scales[s]] * (width // LANES), axis=1)
        summed = jnp.dot(
            links_of(s), gathered[s].reshape(nodes, width), preferred_element_type=jnp.float32
        )
        mixture[s] = ((summed + own_rows(s)) * scale).astype(jnp.bfloat16)

    stores = []

    def settle(s):
        if s == 0:
            fetch.wait()
        mapped = jnp.dot(mixture[s], weight[...], preferred_element_type=jnp.float32)
        rounded = (bend(mapped) + own_rows(s)).astype(jnp.bfloat16)
        out_buf[s] = rounded.reshape(owners, rows, width)
        stores.append(pltpu.make_async_copy(out_buf.at[s], out_hbm.at[:, s], sems.at[s]))
        stores[-1].start()

    stages = (ready, mix, settle)
    for tick in range(snapshots + len(stages) - 1):
        for lag, step in enumerate(stages):
            if 0 <= tick - lag < snapshots:
                step(tick - lag)
    for store in stores:
        store.wait()


def restructure(hidden, staged, w_struct, layer, start, rows):
    snapshots, _, nodes = staged.shape
    owners, _, _, width = hidden[0].shape
    share = nodes // owners
    flops = 2 * snapshots * owners * rows * width * (nodes + width)
    near = pl.BlockSpec(memory_space=pltpu.VMEM)
    return pl.pallas_call(
        functools.partial(restructure_kernel, pieces=len(hidden), layer=layer, start=start),
        out_shape=pltpu.HBM((owners, snapshots, rows, width), jnp.bfloat16),
        in_specs=[near] * (len(hidden) + 1) + [pl.BlockSpec(memory_space=pltpu.HBM)],
        out_specs=pl.BlockSpec(memory_space=pltpu.HBM),
        scratch_shapes=[
            pltpu.VMEM((width, width), jnp.bfloat16),
            pltpu.VMEM((snapshots, owners, share, width), jnp.bfloat16),
            pltpu.VMEM((snapshots, owners * rows, LANES), jnp.float32),
            pltpu.VMEM((snapshots, owners * rows, width), jnp.bfloat16),
            pltpu.VMEM((snapshots, owners, rows, width), jnp.bfloat16),
            pltpu.SemaphoreType.DMA((snapshots + 1,)),
        ],
        compiler_params=pltpu.CompilerParams(vmem_limit_bytes=VMEM_LIMIT),
        cost_estimate=pl.CostEstimate(
            flops=flops, transcendentals=0, bytes_accessed=snapshots * owners * rows * width * 4
        ),
        name=f"structure_{layer}_{start}",
    )(*hidden, staged, in_hbm(w_struct))


def temporal_kernel(
    first_ref,
    x_ref,
    pos_ref,
    gain_ref,
    wq_hbm,
    wk_hbm,
    wv_hbm,
    wo_hbm,
    wu_hbm,
    wd_hbm,
    out_ref,
    wq,
    wk,
    wv,
    wo,
    wu,
    wd,
    sems,
    mixed,
    rows_sum,
    normed,
    queries,
    key_rows,
    values,
    joined,
    order,
    scores,
    weights,
    inner,
    *,
    layer,
    offset,
    first_vertex,
):
    steps, group, width = out_ref.shape
    head_dim = width // HEADS
    pair = 2 * head_dim
    f32 = jnp.float32
    pairs = ((wq_hbm, wq), (wk_hbm, wk), (wv_hbm, wv), (wo_hbm, wo), (wu_hbm, wu), (wd_hbm, wd))
    fetches = [
        pltpu.make_async_copy(source.at[layer], target, sems.at[index])
        for index, (source, target) in enumerate(pairs)
    ]

    @pl.when(pl.program_id(0) == 0)
    def _():
        for fetch in fetches:
            fetch.start()

    row = lax.broadcasted_iota(jnp.int32, (steps, pair), 0)
    lane = lax.broadcasted_iota(jnp.int32, (steps, pair), 1)
    column = lane & (head_dim - 1)
    left = lane < head_dim
    order[...] = jnp.where(row < column, row, jnp.where(row == column, 1 << 20, -1))

    gain_one = gain_ref[layer, 0:1, :]
    gain_two = gain_ref[layer, 1:2, :]
    base = first_vertex + pl.program_id(0) * group
    zero = jnp.zeros((steps, pair), jnp.bfloat16)
    tiles = range(width // LANES)
    half = group // PARTS
    first_row = offset + pl.program_id(0) * group

    def enter(part):
        for tile in tiles:
            mixed[part, tile] = (
                x_ref[
                    :,
                    pl.ds(pl.multiple_of(first_row + part * half, half), half),
                    tile * LANES : (tile + 1) * LANES,
                ]
                .astype(f32)
                .reshape(steps * half, LANES)
            )
        pos = pos_ref[...].astype(f32)
        for v in range(half):
            span = slice(v * steps, (v + 1) * steps)
            parts = [mixed[part, tile, pl.ds(v, steps, stride=half), :] for tile in tiles]
            total = jnp.concatenate(parts, axis=1) + pos
            rows_sum[part, span, :] = total
            normed[part, span, :] = normalise(total, gain_one)

    def project(part):
        rows = normed[part]
        queries[part] = (
            jnp.dot(rows, wq[...], preferred_element_type=f32) * head_dim ** (-0.5)
        ).astype(jnp.bfloat16)
        key_rows[part] = jnp.dot(rows, wk[...], preferred_element_type=f32).astype(jnp.bfloat16)
        values[part] = jnp.dot(rows, wv[...], preferred_element_type=f32).astype(jnp.bfloat16)

    def score(part):
        for v in range(half):
            span = slice(v * steps, (v + 1) * steps)
            for p in range(width // pair):
                lanes = slice(p * pair, (p + 1) * pair)
                q = queries[part, span, lanes]
                stacked = jnp.concatenate(
                    [jnp.where(left, q, zero), jnp.where(left, zero, q)], axis=0
                )
                scores[part, span, lanes] = lax.dot_general(
                    key_rows[part, span, lanes],
                    stacked,
                    (((1,), (1,)), ((), ())),
                    preferred_element_type=f32,
                )

    def soften(part):
        for v in range(half):
            allowed = order[...] >= first_ref[base + part * half + v]
            span = slice(v * steps, (v + 1) * steps)
            for p in range(width // pair):
                lanes = slice(p * pair, (p + 1) * pair)
                seen = jnp.where(allowed, scores[part, span, lanes], -1e30)
                raised = jnp.exp(seen - jnp.max(seen, axis=0, keepdims=True))
                share = 1.0 / jnp.sum(raised, axis=0, keepdims=True)
                weights[part, span, lanes] = (raised * share).astype(jnp.bfloat16)

    def gather(part):
        for v in range(half):
            span = slice(v * steps, (v + 1) * steps)
            for p in range(width // pair):
                lanes = slice(p * pair, (p + 1) * pair)
                both = lax.dot_general(
                    weights[part, span, lanes],
                    values[part, span, lanes],
                    (((0,), (0,)), ((), ())),
                    preferred_element_type=f32,
                )
                joined[part, span, lanes] = jnp.where(left, both[:steps], both[steps:]).astype(
                    jnp.bfloat16
                )

    def attend(part):
        attended = rows_sum[part] + jnp.dot(joined[part], wo[...], preferred_element_type=f32)
        rows_sum[part] = attended

    def second_norm(part):
        normed[part] = normalise(rows_sum[part], gain_two)

    def widen(part):
        inner[part] = jax.nn.gelu(
            jnp.dot(normed[part], wu[...], preferred_element_type=f32)
        ).astype(jnp.bfloat16)

    def finish(part):
        finished = rows_sum[part] + jnp.dot(inner[part], wd[...], preferred_element_type=f32)
        for tile in tiles:
            lanes = slice(tile * LANES, (tile + 1) * LANES)
            for v in range(half):
                mixed[part, tile, pl.ds(v, steps, stride=half), :] = finished[
                    v * steps : (v + 1) * steps, lanes
                ]
            out_ref[:, part * half : (part + 1) * half, lanes] = (
                mixed[part, tile].reshape(steps, half, LANES).astype(jnp.bfloat16)
            )

    def wait_for(some):
        @pl.when(pl.program_id(0) == 0)
        def _():
            for fetch in some:
                fetch.wait()

    def run(*stages):
        for stage in stages:
            for part in range(PARTS):
                stage(part)

    run(enter)
    wait_for(fetches[:3])
    run(project, score, soften, gather)
    wait_for(fetches[3:])
    run(attend, second_norm, widen, finish)


def temporal(rows, first_seen, pos_embed, weights, norm_gain, layer, offset, start, count):
    steps, _, width = rows.shape
    group = 8 * PARTS
    inner = weights[4].shape[-1]
    size = 8 * steps
    flops = 2 * steps * count * width * (4 * width + 2 * inner)
    near = pl.BlockSpec(memory_space=pltpu.VMEM)
    bf16 = jnp.bfloat16
    return pl.pallas_call(
        functools.partial(temporal_kernel, layer=layer, offset=offset, first_vertex=start),
        grid=(count // group,),
        out_shape=pltpu.HBM((steps, count, width), bf16),
        in_specs=[pl.BlockSpec(memory_space=pltpu.SMEM)]
        + [near] * 3
        + [pl.BlockSpec(memory_space=pltpu.HBM)] * len(weights),
        out_specs=pl.BlockSpec((steps, group, width), lambda i: (0, i, 0)),
        scratch_shapes=[pltpu.VMEM(w.shape[1:], bf16) for w in weights]
        + [
            pltpu.SemaphoreType.DMA((len(weights),)),
            pltpu.VMEM((PARTS, width // LANES, size, LANES), jnp.float32),
            pltpu.VMEM((PARTS, size, width), jnp.float32),
            pltpu.VMEM((PARTS, size, width), bf16),
            pltpu.VMEM((PARTS, size, width), bf16),
            pltpu.VMEM((PARTS, size, width), bf16),
            pltpu.VMEM((PARTS, size, width), bf16),
            pltpu.VMEM((PARTS, size, width), bf16),
            pltpu.VMEM((steps, 2 * width // HEADS), jnp.int32),
            pltpu.VMEM((PARTS, size, width), jnp.float32),
            pltpu.VMEM((PARTS, size, width), bf16),
            pltpu.VMEM((PARTS, size, inner), bf16),
        ],
        compiler_params=pltpu.CompilerParams(vmem_limit_bytes=VMEM_LIMIT),
        cost_estimate=pl.CostEstimate(
            flops=flops, transcendentals=0, bytes_accessed=2 * steps * count * width
        ),
        name=f"temporal_{layer}_{start}",
    )(first_seen, rows, pos_embed, norm_gain, *[in_hbm(w) for w in weights])


def deliver_kernel(piece_ref, *refs, start):
    out_hbm, sems = refs[-2:]
    owners, snapshots, rows, _ = piece_ref.shape
    stores = [
        pltpu.make_async_copy(
            piece_ref.at[:, s], out_hbm.at[s, :, start : start + rows], sems.at[s]
        )
        for s in range(snapshots)
    ]
    for store in stores:
        store.start()
    for store in stores:
        store.wait()


def deliver(piece, target, start, share):
    owners, snapshots, _, width = piece.shape
    far = pl.BlockSpec(memory_space=pltpu.HBM)
    operands = [piece] if target is None else [piece, target]
    return pl.pallas_call(
        functools.partial(deliver_kernel, start=start),
        out_shape=pltpu.HBM((snapshots, owners, share, width), piece.dtype),
        in_specs=[pl.BlockSpec(memory_space=pltpu.VMEM)] + [far] * (len(operands) - 1),
        out_specs=far,
        scratch_shapes=[pltpu.SemaphoreType.DMA((snapshots,))],
        input_output_aliases={} if target is None else {1: 0},
        compiler_params=pltpu.CompilerParams(vmem_limit_bytes=VMEM_LIMIT),
        cost_estimate=pl.CostEstimate(
            flops=0, transcendentals=0, bytes_accessed=2 * piece.size * 2
        ),
        name=f"deliver_{start}",
    )(*operands)


def on_device(
    features,
    adjacency,
    first_seen,
    pos_embed,
    w_struct,
    w_query,
    w_key,
    w_value,
    w_out,
    w_up,
    w_down,
    norm_gain,
    *,
    owners,
):
    snapshots, nodes, width = features.shape

    def exchange(array):
        return lax.all_to_all(array, "snap", split_axis=0, concat_axis=0, tiled=True)

    weights = (w_query, w_key, w_value, w_out, w_up, w_down)
    hidden = [features]
    for layer in range(BLOCKS):
        arrived = []
        start = 0
        for rows in OUTWARD:
            if layer == 0 or start > 0:
                piece = structure(hidden, adjacency, w_struct, layer, start, rows, owners)
            else:
                piece = restructure(hidden, staged, w_struct, layer, start, rows)
            piece = exchange(piece)
            arrived.append((start, piece.reshape(owners * snapshots, rows, width)))
            start += rows
        hidden = []
        start = 0
        for rows in HOMEWARD:
            at, piece = [item for item in arrived if item[0] <= start][-1]
            finished = temporal(
                piece, first_seen, pos_embed, weights, norm_gain, layer, start - at, start, rows
            )
            hidden.append(exchange(finished.reshape(owners, snapshots, rows, width)))
            start += rows
        if layer + 1 < BLOCKS:
            staged = stage(adjacency, owners, OUTWARD[0], finished)
    result = None
    start = 0
    for piece in hidden:
        result = deliver(piece, result, start, nodes // owners)
        start += piece.shape[2]
    return result.reshape(snapshots, nodes, width)


def solution(mesh):
    in_specs = (
        P("snap", "clus", None),
        P("snap", "clus", None),
        P(("clus", "snap")),
        P(),
        P(),
        P(),
        P(),
        P(),
        P(),
        P(),
        P(),
        P(),
    )
    out_specs = P("snap", "clus", None)
    return jax.shard_map(
        functools.partial(on_device, owners=mesh.shape["snap"]),
        mesh=mesh,
        in_specs=in_specs,
        out_specs=out_specs,
        check_vma=False,
    )
```

```python
import functools

import jax
import jax.numpy as jnp
from jax import lax
from jax.experimental import pallas as pl
from jax.experimental.pallas import tpu as pltpu
from jax.sharding import PartitionSpec as P

HEADS = 8
BLOCKS = 2
PARTS = 1
OUTWARD = (16, 16)
HOMEWARD = (16, 16)
LANES = 128
VMEM_LIMIT = 32 * 1024 * 1024


def in_hbm(array):
    return pltpu.with_memory_space_constraint(array, pltpu.HBM)


def normalise(rows, gain):
    average = jnp.mean(rows, axis=-1, keepdims=True)
    centred = rows - average
    spread = jnp.mean(centred * centred, axis=-1, keepdims=True)
    return (centred * lax.rsqrt(spread + 1e-05) * gain).astype(jnp.bfloat16)


def bend(mapped):
    return jnp.where(mapped > 0, mapped, jnp.exp(jnp.minimum(mapped, 0.0)) - 1.0)


def structure_kernel(*refs, pieces, layer, start):
    hidden_hbm = refs[:pieces]
    links_hbm, weight_hbm, out_hbm, hidden_buf, links_buf, weight, out_buf, *rest = refs[pieces:]
    scales, narrow, mixture, sems = rest
    snapshots, owners, rows, width = out_buf.shape
    nodes = links_buf.shape[-1]
    share = nodes // owners
    loads = []
    for s in range(snapshots):
        group = []
        below = 0
        for index, ref in enumerate(hidden_hbm):
            count = share if ref.ndim == 3 else ref.shape[2]
            if ref.ndim == 3:
                source, target = ref.at[s], hidden_buf.at[s]
            else:
                source, target = ref.at[:, s], hidden_buf.at[s, :, below : below + count]
            group.append(pltpu.make_async_copy(source, target, sems.at[s, index]))
            below += count
        group.append(
            pltpu.make_async_copy(
                links_hbm.at[s, :, start : start + rows], links_buf.at[s], sems.at[s, pieces]
            )
        )
        loads.append(group)
    fetch = pltpu.make_async_copy(weight_hbm.at[layer], weight, sems.at[snapshots, 0])
    for index, group in enumerate(loads):
        for load in group:
            load.start()
        if index == 0:
            fetch.start()
    stores = []

    def own_rows(s):
        if hidden_buf.ndim == 3:
            own = hidden_buf[s].reshape(owners, share, width)[:, start : start + rows]
        else:
            own = hidden_buf[s, :, start : start + rows, :]
        return own.reshape(owners * rows, width).astype(jnp.float32)

    def ready(s):
        for load in loads[s]:
            load.wait()
        if s == 0:
            fetch.wait()
        links = links_buf[s].reshape(owners * rows, nodes).astype(jnp.float32)
        scale = 1.0 / (1.0 + jnp.sum(links, axis=1, keepdims=True))
        scales[s] = jnp.broadcast_to(scale, (owners * rows, LANES))
        narrow[s] = links.astype(jnp.bfloat16)

    def mix(s):
        summed = jnp.dot(
            narrow[s], hidden_buf[s].reshape(nodes, width), preferred_element_type=jnp.float32
        )
        scale = jnp.concatenate([scales[s]] * (width // LANES), axis=1)
        mixture[s] = ((summed + own_rows(s)) * scale).astype(jnp.bfloat16)

    def settle(s):
        mapped = jnp.dot(mixture[s], weight[...], preferred_element_type=jnp.float32)
        rounded = (bend(mapped) + own_rows(s)).astype(jnp.bfloat16)
        out_buf[s] = rounded.reshape(owners, rows, width)
        stores.append(
            pltpu.make_async_copy(out_buf.at[s], out_hbm.at[:, s], sems.at[snapshots, s + 1])
        )
        stores[-1].start()

    stages = (ready, mix, settle)
    for tick in range(snapshots + len(stages) - 1):
        for lag, step in enumerate(stages):
            if 0 <= tick - lag < snapshots:
                step(tick - lag)
    for store in stores:
        store.wait()


def structure(hidden, adjacency, w_struct, layer, start, rows, owners):
    hidden = hidden if isinstance(hidden, (list, tuple)) else [hidden]
    snapshots, nodes, _ = adjacency.shape
    width = w_struct.shape[-1]
    share = nodes // owners
    links = adjacency.reshape(snapshots, owners, share, nodes)
    near = [in_hbm(h) if h.ndim == 3 else h for h in hidden]
    flops = 2 * snapshots * owners * rows * width * (nodes + width)
    far = pl.BlockSpec(memory_space=pltpu.HBM)
    if hidden[0].ndim == 3:
        hidden_shape = (snapshots, nodes, width)
    else:
        hidden_shape = (snapshots, owners, share, width)
    return pl.pallas_call(
        functools.partial(structure_kernel, pieces=len(hidden), layer=layer, start=start),
        out_shape=pltpu.HBM((owners, snapshots, rows, width), jnp.bfloat16),
        in_specs=[pl.BlockSpec(memory_space=pl.ANY)] * len(hidden) + [far] * 2,
        out_specs=far,
        scratch_shapes=[
            pltpu.VMEM(hidden_shape, jnp.bfloat16),
            pltpu.VMEM((snapshots, owners, rows, nodes), adjacency.dtype),
            pltpu.VMEM((width, width), jnp.bfloat16),
            pltpu.VMEM((snapshots, owners, rows, width), jnp.bfloat16),
            pltpu.VMEM((snapshots, owners * rows, LANES), jnp.float32),
            pltpu.VMEM((snapshots, owners * rows, nodes), jnp.bfloat16),
            pltpu.VMEM((snapshots, owners * rows, width), jnp.bfloat16),
            pltpu.SemaphoreType.DMA((snapshots + 1, snapshots + 1)),
        ],
        compiler_params=pltpu.CompilerParams(vmem_limit_bytes=VMEM_LIMIT),
        cost_estimate=pl.CostEstimate(
            flops=flops, transcendentals=0, bytes_accessed=snapshots * nodes * nodes * 8
        ),
        name=f"structure_{layer}_{start}",
    )(*near, in_hbm(links), in_hbm(w_struct))


def stage_kernel(links_hbm, after_hbm, staged_ref, whole, sems):
    del after_hbm
    snapshots, owners, rows, nodes = whole.shape
    loads = [
        pltpu.make_async_copy(links_hbm.at[s, :, 0:rows], whole.at[s], sems.at[s])
        for s in range(snapshots)
    ]
    for load in loads:
        load.start()
    for s in range(snapshots):
        loads[s].wait()
        links = whole[s].reshape(owners * rows, nodes)
        staged_ref[s] = links.astype(jnp.float32).astype(jnp.bfloat16)


def stage(adjacency, owners, rows, after):
    snapshots, nodes, _ = adjacency.shape
    far = pl.BlockSpec(memory_space=pltpu.HBM)
    links = adjacency.reshape(snapshots, owners, nodes // owners, nodes)
    return pl.pallas_call(
        stage_kernel,
        out_shape=pltpu.VMEM((snapshots, owners * rows, nodes), jnp.bfloat16),
        in_specs=[far] * 2,
        out_specs=pl.BlockSpec(memory_space=pltpu.VMEM),
        scratch_shapes=[
            pltpu.VMEM((snapshots, owners, rows, nodes), adjacency.dtype),
            pltpu.SemaphoreType.DMA((snapshots,)),
        ],
        compiler_params=pltpu.CompilerParams(vmem_limit_bytes=VMEM_LIMIT),
        cost_estimate=pl.CostEstimate(
            flops=0, transcendentals=0, bytes_accessed=adjacency.size * 3
        ),
        name="stage",
    )(in_hbm(links), in_hbm(after))


def restructure_kernel(*refs, pieces, layer, start):
    hidden_refs = refs[:pieces]
    staged_ref, weight_hbm, out_hbm, weight, gathered, scales, mixture, out_buf, sems = refs[pieces:]
    snapshots, owners, rows, width = out_buf.shape
    nodes = staged_ref.shape[-1]
    chosen = slice(start, start + rows)
    fetch = pltpu.make_async_copy(weight_hbm.at[layer], weight, sems.at[snapshots])
    fetch.start()

    def links_of(s):
        return staged_ref[s]

    def ready(s):
        below = 0
        for ref in hidden_refs:
            count = ref.shape[2]
            gathered[s, :, below : below + count, :] = ref[:, s]
            below += count
        degree = 1.0 + jnp.sum(links_of(s).astype(jnp.float32), axis=1, keepdims=True)
        scales[s] = jnp.broadcast_to(1.0 / degree, (owners * rows, LANES))

    def own_rows(s):
        return gathered[s, :, chosen, :].reshape(owners * rows, width).astype(jnp.float32)

    def mix(s):
        scale = jnp.concatenate([scales[s]] * (width // LANES), axis=1)
        summed = jnp.dot(
            links_of(s), gathered[s].reshape(nodes, width), preferred_element_type=jnp.float32
        )
        mixture[s] = ((summed + own_rows(s)) * scale).astype(jnp.bfloat16)

    stores = []

    def settle(s):
        if s == 0:
            fetch.wait()
        mapped = jnp.dot(mixture[s], weight[...], preferred_element_type=jnp.float32)
        rounded = (bend(mapped) + own_rows(s)).astype(jnp.bfloat16)
        out_buf[s] = rounded.reshape(owners, rows, width)
        stores.append(pltpu.make_async_copy(out_buf.at[s], out_hbm.at[:, s], sems.at[s]))
        stores[-1].start()

    stages = (ready, mix, settle)
    for tick in range(snapshots + len(stages) - 1):
        for lag, step in enumerate(stages):
            if 0 <= tick - lag < snapshots:
                step(tick - lag)
    for store in stores:
        store.wait()


def restructure(hidden, staged, w_struct, layer, start, rows):
    snapshots, _, nodes = staged.shape
    owners, _, _, width = hidden[0].shape
    share = nodes // owners
    flops = 2 * snapshots * owners * rows * width * (nodes + width)
    near = pl.BlockSpec(memory_space=pltpu.VMEM)
    return pl.pallas_call(
        functools.partial(restructure_kernel, pieces=len(hidden), layer=layer, start=start),
        out_shape=pltpu.HBM((owners, snapshots, rows, width), jnp.bfloat16),
        in_specs=[near] * (len(hidden) + 1) + [pl.BlockSpec(memory_space=pltpu.HBM)],
        out_specs=pl.BlockSpec(memory_space=pltpu.HBM),
        scratch_shapes=[
            pltpu.VMEM((width, width), jnp.bfloat16),
            pltpu.VMEM((snapshots, owners, share, width), jnp.bfloat16),
            pltpu.VMEM((snapshots, owners * rows, LANES), jnp.float32),
            pltpu.VMEM((snapshots, owners * rows, width), jnp.bfloat16),
            pltpu.VMEM((snapshots, owners, rows, width), jnp.bfloat16),
            pltpu.SemaphoreType.DMA((snapshots + 1,)),
        ],
        compiler_params=pltpu.CompilerParams(vmem_limit_bytes=VMEM_LIMIT),
        cost_estimate=pl.CostEstimate(
            flops=flops, transcendentals=0, bytes_accessed=snapshots * owners * rows * width * 4
        ),
        name=f"structure_{layer}_{start}",
    )(*hidden, staged, in_hbm(w_struct))


def temporal_kernel(
    first_ref,
    x_ref,
    pos_ref,
    gain_ref,
    wq_hbm,
    wk_hbm,
    wv_hbm,
    wo_hbm,
    wu_hbm,
    wd_hbm,
    out_ref,
    wq,
    wk,
    wv,
    wo,
    wu,
    wd,
    sems,
    mixed,
    rows_sum,
    normed,
    queries,
    key_rows,
    values,
    joined,
    order,
    scores,
    weights,
    inner,
    *,
    layer,
    offset,
    first_vertex,
):
    steps, group, width = out_ref.shape
    head_dim = width // HEADS
    pair = 2 * head_dim
    f32 = jnp.float32
    pairs = ((wq_hbm, wq), (wk_hbm, wk), (wv_hbm, wv), (wo_hbm, wo), (wu_hbm, wu), (wd_hbm, wd))
    fetches = [
        pltpu.make_async_copy(source.at[layer], target, sems.at[index])
        for index, (source, target) in enumerate(pairs)
    ]

    @pl.when(pl.program_id(0) == 0)
    def _():
        for fetch in fetches:
            fetch.start()

    row = lax.broadcasted_iota(jnp.int32, (steps, pair), 0)
    lane = lax.broadcasted_iota(jnp.int32, (steps, pair), 1)
    column = lane & (head_dim - 1)
    left = lane < head_dim
    order[...] = jnp.where(row < column, row, jnp.where(row == column, 1 << 20, -1))

    gain_one = gain_ref[layer, 0:1, :]
    gain_two = gain_ref[layer, 1:2, :]
    base = first_vertex + pl.program_id(0) * group
    zero = jnp.zeros((steps, pair), jnp.bfloat16)
    tiles = range(width // LANES)
    half = group // PARTS
    first_row = offset + pl.program_id(0) * group

    def enter(part):
        for tile in tiles:
            mixed[part, tile] = (
                x_ref[
                    :,
                    pl.ds(pl.multiple_of(first_row + part * half, half), half),
                    tile * LANES : (tile + 1) * LANES,
                ]
                .astype(f32)
                .reshape(steps * half, LANES)
            )
        pos = pos_ref[...].astype(f32)
        for v in range(half):
            span = slice(v * steps, (v + 1) * steps)
            parts = [mixed[part, tile, pl.ds(v, steps, stride=half), :] for tile in tiles]
            total = jnp.concatenate(parts, axis=1) + pos
            rows_sum[part, span, :] = total
            normed[part, span, :] = normalise(total, gain_one)

    def project(part):
        rows = normed[part]
        queries[part] = (
            jnp.dot(rows, wq[...], preferred_element_type=f32) * head_dim ** (-0.5)
        ).astype(jnp.bfloat16)
        key_rows[part] = jnp.dot(rows, wk[...], preferred_element_type=f32).astype(jnp.bfloat16)
        values[part] = jnp.dot(rows, wv[...], preferred_element_type=f32).astype(jnp.bfloat16)

    def score(part):
        for v in range(half):
            span = slice(v * steps, (v + 1) * steps)
            for p in range(width // pair):
                lanes = slice(p * pair, (p + 1) * pair)
                q = queries[part, span, lanes]
                stacked = jnp.concatenate(
                    [jnp.where(left, q, zero), jnp.where(left, zero, q)], axis=0
                )
                scores[part, span, lanes] = lax.dot_general(
                    key_rows[part, span, lanes],
                    stacked,
                    (((1,), (1,)), ((), ())),
                    preferred_element_type=f32,
                )

    def soften(part):
        for v in range(half):
            allowed = order[...] >= first_ref[base + part * half + v]
            span = slice(v * steps, (v + 1) * steps)
            for p in range(width // pair):
                lanes = slice(p * pair, (p + 1) * pair)
                seen = jnp.where(allowed, scores[part, span, lanes], -1e30)
                raised = jnp.exp(seen - jnp.max(seen, axis=0, keepdims=True))
                share = 1.0 / jnp.sum(raised, axis=0, keepdims=True)
                weights[part, span, lanes] = (raised * share).astype(jnp.bfloat16)

    def gather(part):
        for v in range(half):
            span = slice(v * steps, (v + 1) * steps)
            for p in range(width // pair):
                lanes = slice(p * pair, (p + 1) * pair)
                both = lax.dot_general(
                    weights[part, span, lanes],
                    values[part, span, lanes],
                    (((0,), (0,)), ((), ())),
                    preferred_element_type=f32,
                )
                joined[part, span, lanes] = jnp.where(left, both[:steps], both[steps:]).astype(
                    jnp.bfloat16
                )

    def attend(part):
        attended = rows_sum[part] + jnp.dot(joined[part], wo[...], preferred_element_type=f32)
        rows_sum[part] = attended

    def second_norm(part):
        normed[part] = normalise(rows_sum[part], gain_two)

    def widen(part):
        inner[part] = jax.nn.gelu(
            jnp.dot(normed[part], wu[...], preferred_element_type=f32)
        ).astype(jnp.bfloat16)

    def finish(part):
        finished = rows_sum[part] + jnp.dot(inner[part], wd[...], preferred_element_type=f32)
        for tile in tiles:
            lanes = slice(tile * LANES, (tile + 1) * LANES)
            for v in range(half):
                mixed[part, tile, pl.ds(v, steps, stride=half), :] = finished[
                    v * steps : (v + 1) * steps, lanes
                ]
            out_ref[:, part * half : (part + 1) * half, lanes] = (
                mixed[part, tile].reshape(steps, half, LANES).astype(jnp.bfloat16)
            )

    def wait_for(some):
        @pl.when(pl.program_id(0) == 0)
        def _():
            for fetch in some:
                fetch.wait()

    def run(*stages):
        for stage in stages:
            for part in range(PARTS):
                stage(part)

    run(enter)
    wait_for(fetches[:3])
    run(project, score, soften, gather)
    wait_for(fetches[3:])
    run(attend, second_norm, widen, finish)


def temporal(rows, first_seen, pos_embed, weights, norm_gain, layer, offset, start, count):
    steps, _, width = rows.shape
    group = 8 * PARTS
    inner = weights[4].shape[-1]
    size = 8 * steps
    flops = 2 * steps * count * width * (4 * width + 2 * inner)
    near = pl.BlockSpec(memory_space=pltpu.VMEM)
    bf16 = jnp.bfloat16
    return pl.pallas_call(
        functools.partial(temporal_kernel, layer=layer, offset=offset, first_vertex=start),
        grid=(count // group,),
        out_shape=pltpu.HBM((steps, count, width), bf16),
        in_specs=[pl.BlockSpec(memory_space=pltpu.SMEM)]
        + [near] * 3
        + [pl.BlockSpec(memory_space=pltpu.HBM)] * len(weights),
        out_specs=pl.BlockSpec((steps, group, width), lambda i: (0, i, 0)),
        scratch_shapes=[pltpu.VMEM(w.shape[1:], bf16) for w in weights]
        + [
            pltpu.SemaphoreType.DMA((len(weights),)),
            pltpu.VMEM((PARTS, width // LANES, size, LANES), jnp.float32),
            pltpu.VMEM((PARTS, size, width), jnp.float32),
            pltpu.VMEM((PARTS, size, width), bf16),
            pltpu.VMEM((PARTS, size, width), bf16),
            pltpu.VMEM((PARTS, size, width), bf16),
            pltpu.VMEM((PARTS, size, width), bf16),
            pltpu.VMEM((PARTS, size, width), bf16),
            pltpu.VMEM((steps, 2 * width // HEADS), jnp.int32),
            pltpu.VMEM((PARTS, size, width), jnp.float32),
            pltpu.VMEM((PARTS, size, width), bf16),
            pltpu.VMEM((PARTS, size, inner), bf16),
        ],
        compiler_params=pltpu.CompilerParams(vmem_limit_bytes=VMEM_LIMIT),
        cost_estimate=pl.CostEstimate(
            flops=flops, transcendentals=0, bytes_accessed=2 * steps * count * width
        ),
        name=f"temporal_{layer}_{start}",
    )(first_seen, rows, pos_embed, norm_gain, *[in_hbm(w) for w in weights])


def deliver_kernel(piece_ref, *refs, start):
    out_hbm, sems = refs[-2:]
    owners, snapshots, rows, _ = piece_ref.shape
    half = owners // 2
    stores = [
        pltpu.make_async_copy(
            piece_ref.at[part * half : (part + 1) * half, s],
            out_hbm.at[s, part * half : (part + 1) * half, start : start + rows],
            sems.at[s, part],
        )
        for s in range(snapshots)
        for part in range(2)
    ]
    for store in stores:
        store.start()
    for store in stores:
        store.wait()


def deliver(piece, target, start, share):
    owners, snapshots, _, width = piece.shape
    far = pl.BlockSpec(memory_space=pltpu.HBM)
    operands = [piece] if target is None else [piece, target]
    return pl.pallas_call(
        functools.partial(deliver_kernel, start=start),
        out_shape=pltpu.HBM((snapshots, owners, share, width), piece.dtype),
        in_specs=[pl.BlockSpec(memory_space=pltpu.VMEM)] + [far] * (len(operands) - 1),
        out_specs=far,
        scratch_shapes=[pltpu.SemaphoreType.DMA((snapshots, 2))],
        input_output_aliases={} if target is None else {1: 0},
        compiler_params=pltpu.CompilerParams(vmem_limit_bytes=VMEM_LIMIT),
        cost_estimate=pl.CostEstimate(
            flops=0, transcendentals=0, bytes_accessed=2 * piece.size * 2
        ),
        name=f"deliver_{start}",
    )(*operands)


def on_device(
    features,
    adjacency,
    first_seen,
    pos_embed,
    w_struct,
    w_query,
    w_key,
    w_value,
    w_out,
    w_up,
    w_down,
    norm_gain,
    *,
    owners,
):
    snapshots, nodes, width = features.shape

    def exchange(array):
        return lax.all_to_all(array, "snap", split_axis=0, concat_axis=0, tiled=True)

    weights = (w_query, w_key, w_value, w_out, w_up, w_down)
    hidden = [features]
    for layer in range(BLOCKS):
        arrived = []
        start = 0
        for rows in OUTWARD:
            if layer == 0 or start > 0:
                piece = structure(hidden, adjacency, w_struct, layer, start, rows, owners)
            else:
                piece = restructure(hidden, staged, w_struct, layer, start, rows)
            piece = exchange(piece)
            arrived.append((start, piece.reshape(owners * snapshots, rows, width)))
            start += rows
        hidden = []
        start = 0
        for rows in HOMEWARD:
            at, piece = [item for item in arrived if item[0] <= start][-1]
            finished = temporal(
                piece, first_seen, pos_embed, weights, norm_gain, layer, start - at, start, rows
            )
            hidden.append(exchange(finished.reshape(owners, snapshots, rows, width)))
            start += rows
        if layer + 1 < BLOCKS:
            staged = stage(adjacency, owners, OUTWARD[0], finished)
    result = None
    start = 0
    for piece in hidden:
        result = deliver(piece, result, start, nodes // owners)
        start += piece.shape[2]
    return result.reshape(snapshots, nodes, width)


def solution(mesh):
    in_specs = (
        P("snap", "clus", None),
        P("snap", "clus", None),
        P(("clus", "snap")),
        P(),
        P(),
        P(),
        P(),
        P(),
        P(),
        P(),
        P(),
        P(),
    )
    out_specs = P("snap", "clus", None)
    return jax.shard_map(
        functools.partial(on_device, owners=mesh.shape["snap"]),
        mesh=mesh,
        in_specs=in_specs,
        out_specs=out_specs,
        check_vma=False,
    )
```
